32 devices in a mesh: seq: 4 (over y, x), batch: 8 (over z, core).
Axes of the slice: x: 2, y: 2, z: 4, core: 2. Of those that a mesh axis runs over, the one named last changes fastest.
Arguments:
- tokens: bfloat16 [8, 1024, 2048], P('batch', 'seq'), may hold values from -6 to 6
- cotangent: bfloat16 [8, 1024, 2048], P('batch', 'seq'), may hold values from -6 to 6
- segment_ids: int32 [8, 1024], P('batch'), may hold values from 0 to 4, as said below
- positions: int32 [8, 1024], P('batch'), may hold values from 0 to 511, as said below
- attn_gain: float32 [2048], replicated, may hold values from 0.5 to 1.5
- qkv_weight: bfloat16 [2048, 2560], P('batch'), may hold values from -0.125 to 0.125
- out_weight: bfloat16 [2048, 2048], P('batch'), may hold values from -0.75 to 0.75
- mlp_gain: float32 [2048], replicated, may hold values from 0.5 to 1.5
- gate_up_weight: bfloat16 [2048, 11264], P('batch'), may hold values from -0.125 to 0.125
- down_weight: bfloat16 [5632, 2048], P('batch'), may hold values from -0.078125 to 0.078125
Outputs:
- output: bfloat16 [8, 1024, 2048], P('batch', 'seq')
- tokens_grad: bfloat16 [8, 1024, 2048], P('batch', 'seq')
- attn_gain_grad: float32 [2048], replicated
- qkv_weight_grad: float32 [2048, 2560], P('batch')
- out_weight_grad: float32 [2048, 2048], P('batch')
- mlp_gain_grad: float32 [2048], replicated
- gate_up_weight_grad: float32 [2048, 11264], P('batch')
- down_weight_grad: float32 [5632, 2048], P('batch')
The draws below stay inside these ranges and needn't reach their ends.
Inputs may be any that keep to these rules, and one draw needn't show every extreme that they name: `segment_ids`: within each packed sequence the ids start at 0, rise by one at each new document and never fall; a document has 1 to 512 tokens and never crosses a multiple of 512 tokens; every sequence holds one document of exactly 512 tokens and 5 documents in all. `positions`: A token's position within its document: 0 at the document's first token, rising by one per token; consistent with segment_ids.
All inputs are finite; a program needn't handle non-finite values.
Results may differ from the reference program's by a relative error of at most 0.02.
Values may be sent and summed in bfloat16 or wider, within the bound.
A program may use at most 384 MiB of HBM per device.

```python
import jax
import jax.numpy as jnp
from jax import lax

D = 2048
H = 32
KV = 4
HD = 64
FF = 5632
BLOCK_ROWS = 512
DOC_MAX = 512
SEQ_LEN = 1024
GROUPS = 8
QKV_COLS = 2560
KV_DUP = 4


def packed_rows(key):
    region_count = SEQ_LEN // DOC_MAX

    def one_row(row_key):
        whole_key, cut_key = jax.random.split(row_key)
        whole_region = jax.random.randint(whole_key, (), 0, region_count)

        def region_cuts(region_key):
            order = jax.random.permutation(region_key, DOC_MAX - 1)
            return jnp.sort(order[:3]).astype(jnp.int32) + 1
        cut_table = jax.vmap(region_cuts)(jax.random.split(cut_key, region_count))
        token_index = jnp.arange(SEQ_LEN, dtype=jnp.int32)
        within = jnp.remainder(token_index, DOC_MAX)
        region = token_index // DOC_MAX
        row_cuts = cut_table[region]
        is_cut = jnp.any(within[:, None] == row_cuts, axis=1) & (region != whole_region)
        starts = (within == 0) | is_cut
        segments = jnp.cumsum(starts.astype(jnp.int32)) - 1
        last_start = lax.cummax(jnp.where(starts, token_index, 0), axis=0)
        return (segments.astype(jnp.int32), (token_index - last_start).astype(jnp.int32))
    return jax.vmap(one_row)(jax.random.split(key, GROUPS))


def draw_segment_ids(key, part):
    return packed_rows(jax.random.fold_in(key, 11))[0]


def draw_positions(key, part):
    return packed_rows(jax.random.fold_in(key, 11))[1]


def shard_levels(rng, shape, shards, least, high):
    factor_of, own = 1.0, jax.random.fold_in(rng, 6)
    for position, shards_of in shards:
        draws = jnp.exp(jax.random.uniform(jax.random.fold_in(own, position), (shards_of,), jnp.float32, least / len(shards), high / len(shards)))
        factor_of = factor_of * jnp.repeat(draws, shape[position] // shards_of).reshape([-1 if axis == position else 1 for axis in range(len(shape))])
    return factor_of


def bell_draw(own_key, extent, width, limit, pieces=(), kind=jnp.bfloat16):
    array = jax.random.normal(own_key, extent, jnp.float32) * width
    if len(pieces) > 0:
        array = shard_levels(own_key, extent, pieces, -0.22, 0.18) * array
    return jnp.clip(array, min=-limit, max=limit).astype(kind)


def setup_inputs(seed: int = 0) -> dict:
    streams_of = jax.random.split(jax.random.key(seed), 11)
    return {
        "tokens": bell_draw(streams_of[0], (GROUPS, SEQ_LEN, D), 1.0, 6.0, ((0, 8), (1, 4))),
        "cotangent": bell_draw(streams_of[1], (GROUPS, SEQ_LEN, D), 1.0, 6.0, ((0, 8), (1, 4))),
        "segment_ids": draw_segment_ids(jax.random.fold_in(streams_of[10], 71), 0),
        "positions": draw_positions(jax.random.fold_in(streams_of[10], 71), 0),
        "attn_gain": jnp.clip(1.0 + 0.1 * jax.random.normal(streams_of[4], (D,), jnp.float32), 0.5, 1.5),
        "qkv_weight": bell_draw(streams_of[5], (D, QKV_COLS), D ** -0.5, 0.125, ((0, 8),)),
        "out_weight": bell_draw(streams_of[6], (D, D), (D // 32) ** -0.5, 0.75, ((0, 8),)),
        "mlp_gain": jnp.clip(1.0 + 0.1 * jax.random.normal(streams_of[7], (D,), jnp.float32), 0.5, 1.5),
        "gate_up_weight": bell_draw(streams_of[8], (D, 2 * FF), D ** -0.5, 0.125, ((0, 8),)),
        "down_weight": bell_draw(streams_of[9], (FF, D), FF ** -0.5, 0.078125, ((0, 8),)),
    }


@jax.custom_vjp
def low(v):
    return lax.optimization_barrier(v.astype(jnp.bfloat16)).astype(jnp.float32)

@jax.custom_vjp
def low_back(v):
    return v

def low_keep(v):
    return (low(v), None)

def low_pass(kept, grad):
    return (grad,)

def back_keep(v):
    return (v, None)

def back_low(kept, grad):
    return (low(grad),)
low.defvjp(low_keep, low_pass)
low_back.defvjp(back_keep, back_low)

def matmul(left, right):
    return jnp.dot(left, right, precision=lax.Precision.HIGHEST, preferred_element_type=jnp.float32)

def rms_norm(values, gain_vector):
    inv_rms = lax.rsqrt(lax.optimization_barrier(jnp.mean(values * values, axis=-1, keepdims=True)) + 1e-05)
    return values * inv_rms * gain_vector

def rotary_tables(seq_positions):
    half_dim = HD // 2
    frequency = 10000.0 ** (-jnp.arange(half_dim, dtype=jnp.float32) * 2.0 / HD)
    angles = seq_positions.astype(jnp.float32)[:, None] * frequency[None, :]
    return (jnp.cos(angles)[:, None, :], jnp.sin(angles)[:, None, :])

def rotate(values, cosine, sine_part):
    half_dim = values.shape[-1] // 2
    first_half = values[..., :half_dim]
    second_half = values[..., half_dim:]
    return jnp.concatenate([first_half * cosine - second_half * sine_part, second_half * cosine + first_half * sine_part], axis=-1)

def block_forward(tokens, attn_gain, qkv_weight, out_weight, mlp_gain, gate_up_weight, down_weight, segments, seq_positions):
    normed = low(rms_norm(tokens, attn_gain))
    projected = matmul(normed, qkv_weight)
    queries = low(low_back(projected[:, :D])).reshape(SEQ_LEN, H, HD)
    kv_part = low_back(projected[:, D:]).reshape(SEQ_LEN, 2, KV, HD)
    kv_dup = low(low_back(jnp.repeat(kv_part, KV_DUP // KV, axis=2)))
    cosine, sine_part = rotary_tables(seq_positions)
    queries_rot = low(rotate(queries, cosine, sine_part))
    keys_rot = jnp.repeat(low(rotate(kv_dup[:, 0], cosine, sine_part)), H // KV_DUP, axis=1)
    values_all = jnp.repeat(kv_dup[:, 1], H // KV_DUP, axis=1)
    token_index = jnp.arange(SEQ_LEN, dtype=jnp.int32)

    def attend(block_index):
        row_start = (block_index * BLOCK_ROWS).astype(jnp.int32)
        query_block = lax.dynamic_slice_in_dim(queries_rot, row_start, BLOCK_ROWS, 0)
        query_ids = lax.dynamic_slice_in_dim(token_index, row_start, BLOCK_ROWS, 0)
        query_segments = lax.dynamic_slice_in_dim(segments, row_start, BLOCK_ROWS, 0)
        allowed = (token_index[None, :] <= query_ids[:, None]) & (segments[None, :] == query_segments[:, None])
        scores = jnp.einsum('qhd,khd->hqk', query_block, keys_rot, precision=lax.Precision.HIGHEST, preferred_element_type=jnp.float32)
        scores = low_back(scores * HD ** (-0.5))
        masked = jnp.where(allowed[None], scores, -1e+30)
        soft_rows = low(jax.nn.softmax(masked, axis=-1))
        return jnp.einsum('hqk,khd->qhd', soft_rows, values_all, precision=lax.Precision.HIGHEST, preferred_element_type=jnp.float32)
    attended = lax.map(jax.checkpoint(attend), jnp.arange(SEQ_LEN // BLOCK_ROWS, dtype=jnp.int32))
    attended = low(low_back(attended.reshape(SEQ_LEN, D)))
    residual = tokens + low_back(matmul(attended, out_weight))
    normed_mlp = low(rms_norm(residual, mlp_gain))
    gate_up = low_back(matmul(normed_mlp, gate_up_weight))
    hidden = low(jax.nn.silu(gate_up[:, :FF]) * gate_up[:, FF:])
    return residual + low_back(matmul(hidden, down_weight))

def reference(tokens, cotangent, segment_ids, positions, attn_gain, qkv_weight, out_weight, mlp_gain, gate_up_weight, down_weight):
    weights = (attn_gain.astype(jnp.float32), qkv_weight.astype(jnp.float32), out_weight.astype(jnp.float32), mlp_gain.astype(jnp.float32), gate_up_weight.astype(jnp.float32), down_weight.astype(jnp.float32))

    def per_group(summed, inputs):
        group_tokens, group_cotangent, group_segments, group_positions = inputs

        def forward(values, *params):
            return block_forward(values, *params, group_segments, group_positions)
        output, pullback = jax.vjp(forward, group_tokens.astype(jnp.float32), *weights)
        gradients = pullback(group_cotangent.astype(jnp.float32))
        summed = tuple((running + update for running, update in zip(summed, gradients[1:])))
        return (summed, (output.astype(jnp.bfloat16), gradients[0].astype(jnp.bfloat16)))
    initial = tuple((jnp.zeros_like(weight_array) for weight_array in weights))
    summed, (outputs, token_grads) = lax.scan(per_group, initial, (tokens, cotangent, segment_ids, positions))
    return (outputs, token_grads, summed[0], summed[1], summed[2], summed[3], summed[4], summed[5])
```

```python
import jax
import jax.numpy as jnp
from jax import lax
from jax.sharding import PartitionSpec as P

H = 32
KV = 4
HD = 64
DOC_MAX = 512
F32 = jnp.float32
BF16 = jnp.bfloat16
AXES = ("seq", "batch")


def rms_parts(values, gain_vector):
    inv_rms = lax.rsqrt(jnp.mean(values * values, axis=-1, keepdims=True) + 1e-05)
    return (values * inv_rms * gain_vector, inv_rms)


def norm_back(grad_normed, values, inv_rms, gain_vector):
    weighted = grad_normed * gain_vector
    inner_sum = jnp.mean(weighted * values, axis=-1, keepdims=True)
    return inv_rms * weighted - values * (inv_rms * inv_rms * inv_rms) * inner_sum


def rotary_tables(seq_positions, head_dim):
    half_dim = head_dim // 2
    frequency = 10000.0 ** (-jnp.arange(half_dim, dtype=F32) * 2.0 / head_dim)
    angles = seq_positions.astype(F32)[:, None] * frequency[None, :]
    return (jnp.cos(angles)[:, None, :], jnp.sin(angles)[:, None, :])


def rotate(values, cosine, sine_part):
    half_dim = values.shape[-1] // 2
    first_half = values[..., :half_dim]
    second_half = values[..., half_dim:]
    return jnp.concatenate(
        [
            first_half * cosine - second_half * sine_part,
            second_half * cosine + first_half * sine_part,
        ],
        axis=-1,
    )


def dot(left, right):
    return jnp.dot(left, right, preferred_element_type=F32)


def dot_nt(left, right):
    return lax.dot_general(left, right, (((1,), (1,)), ((), ())), preferred_element_type=F32)


def dot_tn(left, right):
    return lax.dot_general(left, right, (((0,), (0,)), ((), ())), preferred_element_type=F32)


class Links:
    def __init__(self):
        self.seq = lax.axis_size("seq")
        self.batch = lax.axis_size("batch")
        self.chips = self.batch // 2
        self.bits = self.seq.bit_length() - 1
        if self.seq != 1 << self.bits or self.batch % 2:
            raise ValueError("mesh sizes")
        self.s = lax.axis_index("seq")
        place = lax.axis_index("batch")
        self.z = place // 2
        self.core = place % 2
        reverse = jnp.zeros_like(self.s)
        for bit in range(self.bits):
            reverse = reverse + ((self.s >> bit) & 1) * (1 << (self.bits - 1 - bit))
        self.part = jnp.where(self.core == 0, reverse, self.s)

    def send(self, array, target):
        pairs = []
        for z in range(self.chips):
            for core in range(2):
                for s in range(self.seq):
                    tz, tc, ts = target(z, core, s)
                    here, there = z * 2 + core, tz * 2 + tc
                    pairs.append((s * self.batch + here, ts * self.batch + there))
        return lax.ppermute(array, AXES, pairs)

    def up(self, array, shift):
        return self.send(array, lambda z, c, s: ((z + shift) % self.chips, c, s))

    def swap_cores(self, array):
        return self.send(array, lambda z, c, s: (z, 1 - c, s))

    def stage(self, array, step):
        masks = (1 << step, 1 << (self.bits - 1 - step))
        return self.send(array, lambda z, c, s: (z, c, s ^ masks[c]))

    def plane_gather(self, array):
        held = [(0, array)]
        level = [(0, -1, array)]
        while level:
            fresh = [
                (mask ^ (1 << (self.bits - 1 - step)), step, self.stage(one, step))
                for mask, last, one in level
                for step in range(last + 1, self.bits)
            ]
            if not fresh:
                return held
            arrays = yield [one for _, _, one in fresh]
            level = [(mask, step, one) for (mask, step, _), one in zip(fresh, arrays)]
            held = held + [(mask, one) for mask, _, one in level]
        return held

    def total(self, value):
        value = value + self.swap_cores(value)
        for step in range(self.bits):
            value = value + self.stage(value, step)
        step = 1
        while step < self.chips:
            mask = step
            value = value + self.send(value, lambda z, c, s: (z ^ mask, c, s))
            step *= 2
        return value

    def gather(self, shard):
        rows, width = shard.shape
        piece = rows // self.seq
        (mine,) = yield [lax.dynamic_slice(shard, (self.part * piece, 0), (piece, width))]
        along = yield [self.up(mine, -k) for k in range(1, self.chips)]
        held = yield from self.plane_gather(jnp.stack(along))
        whole = jnp.zeros((self.chips, self.seq, piece, width), shard.dtype)
        whole = whole.at[0].set(shard.reshape(self.seq, piece, width))
        for mask, one in held:
            whole = lax.dynamic_update_slice(whole, one[:, None], (1, self.part ^ mask, 0, 0))
        whole = whole.reshape(self.chips * rows, width)
        (other,) = yield [self.swap_cores(whole)]
        return whole, other

    def split(self, values):
        count = values.shape[0]
        rows = values.shape[1] // self.batch
        twice = jnp.concatenate([values, values], axis=1)
        turned = lax.dynamic_slice(twice, (0, self.z * 2 * rows), values.shape)
        turned = turned.reshape(count, self.chips, 2, rows)
        first = turned[:, :, 0].reshape(count, self.chips * rows)
        second = turned[:, :, 1].reshape(count, self.chips * rows)
        even = self.core == 0
        return jnp.where(even, first, second), jnp.where(even, second, first)

    def join(self, own, sibling):
        count = own.shape[0]
        rows = own.shape[1] // self.chips
        even = self.core == 0
        first = jnp.where(even, own, sibling).reshape(count, self.chips, rows)
        second = jnp.where(even, sibling, own).reshape(count, self.chips, rows)
        turned = jnp.stack([first, second], axis=2).reshape(count, self.batch * rows)
        twice = jnp.concatenate([turned, turned], axis=1)
        back = (self.chips - self.z) % self.chips
        return lax.dynamic_slice(twice, (0, back * 2 * rows), turned.shape)

    def weight_gradient(self, pair, grads_out):
        own, sibling = pair
        (away,) = yield [dot_tn(sibling, grads_out).astype(BF16)]
        arrived, held = yield [self.swap_cores(away), dot_tn(own, grads_out).astype(BF16)]
        width = held.shape[1]
        held = held.reshape(self.chips, -1, width)
        arrived = arrived.reshape(held.shape)
        for step in range(self.bits):
            half = held.shape[1] // 2
            shape = (self.chips, half, width)
            bit = (self.part >> (self.bits - 1 - step)) & 1
            keep, leave = [
                (
                    lax.dynamic_slice(held, (0, side * half, 0), shape).astype(F32)
                    + lax.dynamic_slice(arrived, (0, side * half, 0), shape).astype(F32)
                ).astype(BF16)
                for side in (bit, 1 - bit)
            ]
            held, leave = yield [keep, leave]
            (arrived,) = yield [self.stage(leave, step)]
        held = yield list(
            (held.astype(F32) + arrived.astype(F32)).astype(BF16)[k] for k in range(self.chips)
        )
        along = yield [self.up(held[k], k) for k in range(1, self.chips)]
        sums = held[0].astype(F32)
        for one in along:
            sums = sums + one.astype(F32)
        (sums,) = yield [sums.astype(BF16)]
        held = yield from self.plane_gather(sums)
        piece = sums.shape[0]
        whole = jnp.zeros((self.seq, piece, width), F32)
        for mask, one in held:
            whole = lax.dynamic_update_slice(whole, one[None].astype(F32), (self.part ^ mask, 0, 0))
        return whole.reshape(self.seq * piece, width)


class Task:
    def __init__(self, steps):
        self.steps = steps
        self.given = None
        self.result = None
        self.done = False


def run(tasks):
    while any(not task.done for task in tasks):
        wanted = []
        for task in list(tasks):
            if task.done:
                continue
            try:
                asked = task.steps.send(task.given)
                wanted.append((task, asked))
            except StopIteration as stop:
                task.result = stop.value
                task.done = True
        flat = [array for _, asked in wanted for array in asked]
        if flat:
            flat = list(lax.optimization_barrier(tuple(flat)))
        for task, asked in wanted:
            task.given, flat = flat[: len(asked)], flat[len(asked) :]


def local(
    tokens,
    cotangent,
    segment_ids,
    positions,
    attn_gain,
    qkv_weight,
    out_weight,
    mlp_gain,
    gate_up_weight,
    down_weight,
):
    links = Links()
    model_width = tokens.shape[2]
    rows = tokens.shape[1]
    if rows * 2 != DOC_MAX:
        raise ValueError("token shard")
    share = H // KV
    kv_width = KV * HD
    scale_factor = HD ** (-0.5)
    ff_width = gate_up_weight.shape[1] // 2

    tasks = []

    def launch(steps, delay=0):
        def later():
            for _ in range(delay):
                yield []
            return (yield from steps)

        tasks.append(Task(later()))
        return tasks[-1]

    def wait(task):
        while not task.done:
            yield []
        return task.result

    qkv_task = launch(links.gather(qkv_weight))
    out_task = launch(links.gather(out_weight), 1)
    gate_task = launch(links.gather(gate_up_weight[:, :ff_width]), 2)
    up_task = launch(links.gather(gate_up_weight[:, ff_width:]), 3)
    down_task = launch(links.gather(down_weight), 4)

    def product(pair, weights):
        return dot(pair[0], weights[0]) + dot(pair[1], weights[1])

    def main():
        inputs = tokens[0].astype(F32)
        normed, inv_first = rms_parts(inputs, attn_gain)
        normed_pair = yield links.split(normed.astype(BF16))
        qkv_pair = yield from wait(qkv_task)
        projected = product(normed_pair, qkv_pair)

        row_start = links.s * rows
        own_segments = lax.dynamic_slice_in_dim(segment_ids[0], row_start, rows, 0)
        other = links.s ^ 1
        other_segments = lax.dynamic_slice_in_dim(segment_ids[0], other * rows, rows, 0)
        own_positions = lax.dynamic_slice_in_dim(positions[0], row_start, rows, 0)
        cosine, sine_part = rotary_tables(own_positions, HD)
        queries = projected[:, :model_width].astype(BF16).reshape(rows, H, HD)
        queries_rot = rotate(queries.astype(F32), cosine, sine_part).astype(BF16)
        queries_rot = queries_rot.reshape(rows, KV, share, HD)
        keys = projected[:, model_width : model_width + kv_width].astype(BF16).reshape(rows, KV, HD)
        keys_rot = rotate(keys.astype(F32), cosine, sine_part).astype(BF16).reshape(rows, kv_width)
        values = projected[:, model_width + kv_width :].astype(BF16)
        own_kv = jnp.concatenate([keys_rot, values], axis=1)
        own_kv, queries_rot = yield [own_kv, queries_rot]
        (other_kv,) = yield [links.send(own_kv, lambda z, c, s: (z, c, s ^ 1))]
        both_kv = jnp.concatenate([own_kv, other_kv], axis=0)
        all_keys = both_kv[:, :kv_width].reshape(2 * rows, KV, HD)
        all_values = both_kv[:, kv_width:].reshape(2 * rows, KV, HD)
        index = jnp.arange(rows, dtype=jnp.int32)
        allowed = jnp.concatenate(
            [
                (index[None, :] <= index[:, None]) & (own_segments[None, :] == own_segments[:, None]),
                (other < links.s) & (other_segments[None, :] == own_segments[:, None]),
            ],
            axis=1,
        )
        scores = (
            jnp.einsum("qgsd,kgd->gsqk", queries_rot, all_keys, preferred_element_type=F32)
            * scale_factor
        )
        masked = jnp.where(allowed[None, None], scores, -1e30)
        row_max = jnp.max(masked, axis=-1, keepdims=True)
        exps = jnp.exp(masked - row_max)
        probs = exps / jnp.sum(exps, axis=-1, keepdims=True)
        probs_low = probs.astype(BF16)
        attended = jnp.einsum("gsqk,kgd->qgsd", probs_low, all_values, preferred_element_type=F32)
        attended = attended.astype(BF16).reshape(rows, model_width)
        attended, probs, probs_low = yield [attended, probs, probs_low]
        attended_pair = links.split(attended)
        out_pair = yield from wait(out_task)
        residual = inputs + product(attended_pair, out_pair)
        normed_mlp, inv_second = rms_parts(residual, mlp_gain)
        mlp_pair = links.split(normed_mlp.astype(BF16))
        residual, inv_second, *mlp_pair = yield [residual, inv_second, *mlp_pair]
        gate_pair = yield from wait(gate_task)
        (gate_part,) = yield [product(mlp_pair, gate_pair)]
        up_pair = yield from wait(up_task)
        up_part = product(mlp_pair, up_pair)
        sigmoid_gate = jax.nn.sigmoid(gate_part)
        hidden_pair = links.split((gate_part * sigmoid_gate * up_part).astype(BF16))
        up_part, *hidden_pair = yield [up_part, *hidden_pair]

        grad_out = cotangent[0].astype(F32)
        grad_down = cotangent[0]
        down_reduce = launch(links.weight_gradient(hidden_pair, grad_down))
        down_pair = yield from wait(down_task)
        grad_hidden = links.join(dot_nt(grad_down, down_pair[0]), dot_nt(grad_down, down_pair[1]))
        grad_gate = grad_hidden * up_part * sigmoid_gate * (1.0 + gate_part * (1.0 - sigmoid_gate))
        grad_gate = grad_gate.astype(BF16)
        grad_up = (grad_hidden * gate_part * sigmoid_gate).astype(BF16)
        grad_gate, grad_up = yield [grad_gate, grad_up]
        gate_reduce = launch(links.weight_gradient(mlp_pair, grad_gate))
        up_reduce = launch(links.weight_gradient(mlp_pair, grad_up), 2)
        grad_normed_mlp = links.join(
            dot_nt(grad_gate, gate_pair[0]) + dot_nt(grad_up, up_pair[0]),
            dot_nt(grad_gate, gate_pair[1]) + dot_nt(grad_up, up_pair[1]),
        )
        mlp_term = jnp.sum(grad_normed_mlp * residual * inv_second, axis=0)
        grad_resid = grad_out + norm_back(grad_normed_mlp, residual, inv_second, mlp_gain)
        grad_resid, mlp_term, grad_proj = yield [grad_resid, mlp_term, grad_resid.astype(BF16)]
        out_reduce = launch(links.weight_gradient(attended_pair, grad_proj), 1)
        grad_heads = links.join(dot_nt(grad_proj, out_pair[0]), dot_nt(grad_proj, out_pair[1]))
        (grad_heads,) = yield [grad_heads.astype(BF16)]
        grad_heads = grad_heads.reshape(rows, KV, share, HD)

        grad_probs = jnp.einsum("qgsd,kgd->gsqk", grad_heads, all_values, preferred_element_type=F32)
        inner_sum = jnp.sum(probs * grad_probs, axis=-1, keepdims=True)
        grad_scores = (probs * (grad_probs - inner_sum)).astype(BF16)
        grad_queries = (
            jnp.einsum("gsqk,kgd->qgsd", grad_scores, all_keys, preferred_element_type=F32)
            * scale_factor
        )
        grad_keys = (
            jnp.einsum("gsqk,qgsd->kgd", grad_scores, queries_rot, preferred_element_type=F32)
            * scale_factor
        )
        grad_values = jnp.einsum("gsqk,qgsd->kgd", probs_low, grad_heads, preferred_element_type=F32)
        grad_kv = jnp.concatenate(
            [grad_keys.reshape(2 * rows, kv_width), grad_values.reshape(2 * rows, kv_width)], axis=1
        )
        away, grad_kv, grad_queries = yield [grad_kv[rows:].astype(BF16), grad_kv, grad_queries]
        (arrived,) = yield [links.send(away, lambda z, c, s: (z, c, s ^ 1))]
        own_grad_kv = grad_kv[:rows] + arrived.astype(F32)
        back_queries = rotate(grad_queries.reshape(rows, H, HD), cosine, -sine_part)
        back_keys = rotate(own_grad_kv[:, :kv_width].reshape(rows, KV, HD), cosine, -sine_part)
        grad_qkv = jnp.concatenate(
            [
                back_queries.reshape(rows, model_width),
                back_keys.reshape(rows, kv_width),
                own_grad_kv[:, kv_width:],
            ],
            axis=1,
        ).astype(BF16)
        (grad_qkv,) = yield [grad_qkv]
        qkv_reduce = launch(links.weight_gradient(normed_pair, grad_qkv))
        output = (residual + product(hidden_pair, down_pair)).astype(BF16)
        grad_normed = links.join(dot_nt(grad_qkv, qkv_pair[0]), dot_nt(grad_qkv, qkv_pair[1]))
        attn_term = jnp.sum(grad_normed * inputs * inv_first, axis=0)
        tokens_grad = (grad_resid + norm_back(grad_normed, inputs, inv_first, attn_gain)).astype(BF16)
        tokens_grad, attn_term, output = yield [tokens_grad, attn_term, output]
        gains = links.total(jnp.concatenate([attn_term, mlp_term]).reshape(-1, 128)).reshape(-1)
        qkv_grad = yield from wait(qkv_reduce)
        out_grad = yield from wait(out_reduce)
        down_grad = yield from wait(down_reduce)
        gate_grad = yield from wait(gate_reduce)
        up_grad = yield from wait(up_reduce)
        return (
            output[None],
            tokens_grad[None],
            gains[:model_width],
            qkv_grad,
            out_grad,
            gains[model_width:],
            jnp.concatenate([gate_grad, up_grad], axis=1),
            down_grad,
        )

    head = launch(main())
    run(tasks)
    return head.result


def solution(mesh):
    return jax.shard_map(
        local,
        mesh=mesh,
        in_specs=(
            P("batch", "seq", None),
            P("batch", "seq", None),
            P("batch", None),
            P("batch", None),
            P(),
            P("batch", None),
            P("batch", None),
            P(),
            P("batch", None),
            P("batch", None),
        ),
        out_specs=(
            P("batch", "seq", None),
            P("batch", "seq", None),
            P(),
            P("batch", None),
            P("batch", None),
            P(),
            P("batch", None),
            P("batch", None),
        ),
        check_vma=False,
    )
```

```python
import functools

import jax
import jax.numpy as jnp
from jax import lax
from jax.experimental import pallas as pl
from jax.experimental.pallas import tpu as pltpu
from jax.sharding import PartitionSpec as P

H = 32
KV = 4
HD = 64
DOC_MAX = 512
F32 = jnp.float32
BF16 = jnp.bfloat16


def rms_parts(values, gain_vector):
    inv_rms = lax.rsqrt(jnp.mean(values * values, axis=-1, keepdims=True) + 1e-05)
    return (values * inv_rms * gain_vector, inv_rms)


def norm_back(grad_normed, values, inv_rms, gain_vector):
    weighted = grad_normed * gain_vector
    inner_sum = jnp.mean(weighted * values, axis=-1, keepdims=True)
    return inv_rms * weighted - values * (inv_rms * inv_rms * inv_rms) * inner_sum


def rotary_tables(seq_positions, head_dim):
    half_dim = head_dim // 2
    frequency = 10000.0 ** (-jnp.arange(half_dim, dtype=F32) * 2.0 / head_dim)
    angles = seq_positions.astype(F32)[:, None] * frequency[None, :]
    return (jnp.cos(angles)[:, None, :], jnp.sin(angles)[:, None, :])


def rotate(values, cosine, sine_part):
    half_dim = values.shape[-1] // 2
    first_half = values[..., :half_dim]
    second_half = values[..., half_dim:]
    return jnp.concatenate(
        [
            first_half * cosine - second_half * sine_part,
            second_half * cosine + first_half * sine_part,
        ],
        axis=-1,
    )


def dot(left, right):
    return jnp.dot(left, right, preferred_element_type=F32)


def dot_nt(left, right):
    return lax.dot_general(left, right, (((1,), (1,)), ((), ())), preferred_element_type=F32)


def dot_tn(left, right):
    return lax.dot_general(left, right, (((0,), (0,)), ((), ())), preferred_element_type=F32)


class Place:
    def __init__(self, chips, bits):
        self.chips, self.bits = chips, bits
        self.s = lax.axis_index("seq")
        place = lax.axis_index("batch")
        self.z, self.core = place // 2, place % 2
        reverse = 0
        for bit in range(bits):
            reverse = reverse + ((self.s // (1 << bit)) % 2) * (1 << (bits - 1 - bit))
        self.part = reverse + self.core * (self.s - reverse)

    def sibling(self):
        return {"batch": self.z * 2 + 1 - self.core}

    def chip(self, shift):
        return {"batch": ((self.z + shift) % self.chips) * 2 + self.core}

    def partner(self, step):
        first, second = 1 << step, 1 << (self.bits - 1 - step)
        mask = first + self.core * (second - first)
        return {"seq": self.s + mask * (1 - 2 * ((self.s // mask) % 2))}

    def fellows(self):
        found = [self.sibling()] + [self.partner(step) for step in range(self.bits)]
        step = 1
        while step < self.chips:
            found.append({"batch": (self.z + step * (1 - 2 * ((self.z // step) % 2))) * 2 + self.core})
            step *= 2
        return found

    def bit(self, step):
        return (self.part // (1 << (self.bits - 1 - step))) % 2

    def part_of(self, subset):
        part = self.part
        for step in range(self.bits):
            if subset >> step & 1:
                weight = 1 << (self.bits - 1 - step)
                part = part + weight * (1 - 2 * self.bit(step))
        return part


def reduce_kernel(chips, bits, count, terms, small, out, arrived, small_out, *scratch):
    halves = scratch[:bits]
    own, got, along, final = scratch[bits : bits + 4]
    (own_sem, got_sem, core_out, core_in, half_out, half_in, along_out, along_in, spread_out, spread_in, local_sem) = (
        scratch[bits + 4 : -4]
    )
    small_sum, small_got, small_send, small_recv = scratch[-4:]
    here = Place(chips, bits)
    rows, width = own.shape[2], own.shape[3]
    piece = rows >> bits
    slots = own.shape[0]
    seq = 1 << bits

    barrier = pltpu.get_barrier_semaphore()
    peers = [here.sibling()] + [here.partner(i) for i in range(bits)] + [here.chip(k) for k in range(1, chips)]
    fellows = here.fellows()
    for peer in peers:
        pl.semaphore_signal(barrier, inc=1, device_id=peer, device_id_type=pl.DeviceIdType.MESH)
    pl.semaphore_wait(barrier, len(peers))

    def columns(j):
        return pl.ds(pl.multiple_of(j * width, 128), width)

    def core_copy(j):
        return pltpu.make_async_remote_copy(
            src_ref=terms.at[:, 1 - here.core, :, columns(j)],
            dst_ref=arrived.at[j],
            send_sem=core_out.at[j],
            recv_sem=core_in.at[j],
            device_id=here.sibling(),
            device_id_type=pl.DeviceIdType.MESH,
        )

    def own_load(j):
        return pltpu.make_async_copy(terms.at[:, here.core, :, columns(j)], own.at[j % slots], own_sem.at[j])

    def got_load(j):
        return pltpu.make_async_copy(arrived.at[j], got.at[j % 2], got_sem.at[j])

    def offset(step):
        total = 0
        for i in range(step):
            total = total + here.bit(i) * (rows >> (i + 1))
        return total

    def half_copy(j, step):
        half = rows >> (step + 1)
        first = pl.multiple_of(offset(step) + (1 - here.bit(step)) * half, piece)
        return pltpu.make_async_remote_copy(
            src_ref=own.at[j % slots, :, pl.ds(first, half), :],
            dst_ref=halves[step].at[j],
            send_sem=half_out.at[j, step],
            recv_sem=half_in.at[j, step],
            device_id=here.partner(step),
            device_id_type=pl.DeviceIdType.MESH,
        )

    def along_copy(j, k):
        first = pl.multiple_of(offset(bits), piece)
        return pltpu.make_async_remote_copy(
            src_ref=own.at[j % slots, (here.z + k) % chips, pl.ds(first, piece), :],
            dst_ref=along.at[j, k - 1],
            send_sem=along_out.at[j, k - 1],
            recv_sem=along_in.at[j, k - 1],
            device_id=here.chip(k),
            device_id_type=pl.DeviceIdType.MESH,
        )

    def place_of(j, subset):
        return out.at[pl.ds(pl.multiple_of(here.part_of(subset) * piece, piece), piece), columns(j)]

    def spread_copy(j, subset):
        last = subset.bit_length() - 1
        parent = subset ^ (1 << last)
        return pltpu.make_async_remote_copy(
            src_ref=final.at[j] if parent == 0 else place_of(j, parent),
            dst_ref=place_of(j, parent),
            send_sem=spread_out.at[j, subset - 1],
            recv_sem=spread_in.at[j, subset - 1],
            device_id=here.partner(last),
            device_id_type=pl.DeviceIdType.MESH,
        )

    def local_copy(j):
        return pltpu.make_async_copy(final.at[j], place_of(j, 0), local_sem.at[j])

    def level(size):
        return [subset for subset in range(1, seq) if bin(subset).count("1") == size]

    def fresh(j):
        core_copy(j).start()

    def loads(j):
        core_copy(j).wait()
        own_load(j).start()
        got_load(j).start()

    def first_sum(j):
        own_load(j).wait()
        got_load(j).wait()
        block = 32 if rows % 32 == 0 else 16
        blocks = rows // block
        slot = j % slots

        def body(index, carry):
            z = index // blocks
            span = pl.ds(pl.multiple_of((index % blocks) * block, block), block)
            own[slot, z, span, :] = (
                own[slot, z, span, :].astype(F32) + got[j % 2, z, span, :].astype(F32)
            ).astype(BF16)
            return carry

        lax.fori_loop(0, chips * blocks, body, 0)

    def half_sum(j, step):
        half_copy(j, step).wait()
        half = rows >> (step + 1)
        block = 32 if half % 32 == 0 else 16
        blocks = half // block
        slot = j % slots
        start = offset(step + 1)

        def body(index, carry):
            z = index // blocks
            first = (index % blocks) * block
            there = pl.ds(pl.multiple_of(first, block), block)
            span = pl.ds(pl.multiple_of(start + first, block), block)
            own[slot, z, span, :] = (
                own[slot, z, span, :].astype(F32) + halves[step][j, z, there, :].astype(F32)
            ).astype(BF16)
            return carry

        lax.fori_loop(0, chips * blocks, body, 0)

    def send_along(j):
        for k in range(1, chips):
            along_copy(j, k).start()

    def last_sum(j):
        for k in range(1, chips):
            along_copy(j, k).wait()
        block = 16
        slot = j % slots
        start = offset(bits)

        def body(index, carry):
            first = index * block
            there = pl.ds(pl.multiple_of(first, block), block)
            total = own[slot, here.z, pl.ds(pl.multiple_of(start + first, block), block), :].astype(F32)
            for k in range(chips - 1):
                total = total + along[j, k, there, :].astype(F32)
            final[j, there, :] = total.astype(BF16)
            return carry

        lax.fori_loop(0, piece // block, body, 0)
        local_copy(j).start()
        for subset in level(1):
            spread_copy(j, subset).start()

    def pass_on(j, size):
        for subset in level(size):
            spread_copy(j, subset).wait()
        for subset in level(size + 1):
            spread_copy(j, subset).start()

    def small_copy(step):
        return pltpu.make_async_remote_copy(
            src_ref=small_sum.at[step],
            dst_ref=small_got.at[step],
            send_sem=small_send.at[step],
            recv_sem=small_recv.at[step],
            device_id=fellows[step],
            device_id_type=pl.DeviceIdType.MESH,
        )

    def small_step(step):
        if step:
            small_copy(step - 1).wait()
            small_sum[step] = small_sum[step - 1] + small_got[step - 1]
        if step < len(fellows):
            small_copy(step).start()
        else:
            small_out[...] = small_sum[step]

    stages = [fresh, loads, first_sum, lambda j: half_copy(j, 0).start()]
    for step in range(bits):

        def stage(j, step=step):
            half_sum(j, step)
            if step + 1 < bits:
                half_copy(j, step + 1).start()
            else:
                send_along(j)

        stages.append(stage)
    stages.append(last_sum)
    for size in range(1, bits + 1):
        stages.append(lambda j, size=size: pass_on(j, size))
    stages.append(lambda j: local_copy(j).wait())
    order = list(range(3, len(stages))) + [2, 1, 0]

    def round_of(now, carry):
        for step in range(len(fellows) + 1):

            @pl.when(now == step)
            def _(step=step):
                small_step(step)

        for number in order:
            chunk = now - number

            @pl.when((chunk >= 0) & (chunk < count))
            def _(number=number, chunk=chunk):
                stages[number](chunk)

        return carry

    small_sum[0] = small[...]
    lax.fori_loop(0, count + len(stages) - 1, round_of, 0)


def reduced(terms, small, chips, bits, count, number):
    rows, width = terms.shape[0] // (2 * chips), terms.shape[1]
    seq, wide = 1 << bits, width // count
    piece = rows // seq
    slots = bits + 5
    dma = pltpu.SemaphoreType.DMA
    steps = 1 + bits + (chips - 1).bit_length()
    out, _, small_out = pl.pallas_call(
        functools.partial(reduce_kernel, chips, bits, count),
        out_shape=(
            jax.ShapeDtypeStruct((rows, width), BF16),
            jax.ShapeDtypeStruct((count, chips, rows, wide), BF16),
            jax.ShapeDtypeStruct(small.shape, F32),
        ),
        in_specs=[pl.BlockSpec(memory_space=pl.ANY), pl.BlockSpec(memory_space=pltpu.VMEM)],
        out_specs=(
            pl.BlockSpec(memory_space=pl.ANY),
            pl.BlockSpec(memory_space=pl.ANY),
            pl.BlockSpec(memory_space=pltpu.VMEM),
        ),
        scratch_shapes=[pltpu.VMEM((count, chips, rows >> (step + 1), wide), BF16) for step in range(bits)]
        + [
            pltpu.VMEM((slots, chips, rows, wide), BF16),
            pltpu.VMEM((2, chips, rows, wide), BF16),
            pltpu.VMEM((count, chips - 1, piece, wide), BF16),
            pltpu.VMEM((count, piece, wide), BF16),
            dma((count,)),
            dma((count,)),
            dma((count,)),
            dma((count,)),
            dma((count, bits)),
            dma((count, bits)),
            dma((count, chips - 1)),
            dma((count, chips - 1)),
            dma((count, seq - 1)),
            dma((count, seq - 1)),
            dma((count,)),
            pltpu.VMEM((steps + 1,) + small.shape, F32),
            pltpu.VMEM((steps,) + small.shape, F32),
            dma((steps,)),
            dma((steps,)),
        ],
        compiler_params=pltpu.CompilerParams(
            collective_id=number, has_side_effects=True, vmem_limit_bytes=62 * 1024 * 1024
        ),
        cost_estimate=pl.CostEstimate(flops=0, bytes_accessed=800_000_000, transcendentals=0),
    )(terms.reshape(chips, 2, rows, width), small)
    return out, small_out


def gather_kernel(chips, bits, units, weights, *refs):
    shards, wholes = refs[:weights], refs[weights : 2 * weights]
    held = refs[2 * weights : 3 * weights]
    (in_sem, own_sem, along_out, along_in, spread_out, spread_in, turn_out, turn_in) = refs[3 * weights :]
    here = Place(chips, bits)
    seq = 1 << bits

    barrier = pltpu.get_barrier_semaphore()
    peers = [here.sibling()] + [here.partner(i) for i in range(bits)] + [here.chip(k) for k in range(1, chips)]
    for peer in peers:
        pl.semaphore_signal(barrier, inc=1, device_id=peer, device_id_type=pl.DeviceIdType.MESH)
    pl.semaphore_wait(barrier, len(peers))

    def rows_of(unit, shift):
        which, first, width = units[unit]
        count = shards[which].shape[0]
        row = (((here.z - shift) % chips) * 2 + here.core) * count
        return which, row, count, first, width

    def piece_of(unit, shift, subset):
        which, row, count, first, width = rows_of(unit, shift)
        part = here.part_of(subset)
        if (count // seq) % 16 == 0:
            size = count // seq
            return which, pl.ds(pl.multiple_of(row + part * size, 16), size), pl.ds(first, width)
        size = width // seq
        return which, pl.ds(pl.multiple_of(row, 16), count), pl.ds(pl.multiple_of(first + part * size, 128), size)

    def remote(source, target, sems, index, device):
        return pltpu.make_async_remote_copy(
            src_ref=source,
            dst_ref=target,
            send_sem=sems[0].at[index],
            recv_sem=sems[1].at[index],
            device_id=device,
            device_id_type=pl.DeviceIdType.MESH,
        )

    def along(unit, k):
        which, row, count, first, width = rows_of(unit, 0)
        _, there, columns = piece_of(unit, 0, 0)
        part = here.part
        if (count // seq) % 16 == 0:
            size = count // seq
            source = shards[which].at[pl.ds(pl.multiple_of(part * size, 16), size), columns]
        else:
            source = shards[which].at[:, columns]
        return remote(source, wholes[which].at[there, columns], (along_out, along_in), (unit, k - 1), here.chip(k))

    def spread(unit, k, subset):
        last = subset.bit_length() - 1
        which, there, columns = piece_of(unit, k, subset ^ (1 << last))
        region = wholes[which].at[there, columns]
        return remote(region, region, (spread_out, spread_in), (unit, k - 1, subset - 1), here.partner(last))

    def turn(unit, k):
        which, row, count, first, width = rows_of(unit, k)
        there = pl.ds(pl.multiple_of(row, 16), count)
        region = wholes[which].at[there, pl.ds(first, width)]
        source = region if k else shards[which].at[:, pl.ds(first, width)]
        return remote(source, region, (turn_out, turn_in), (unit, k), here.sibling())

    def load(which):
        return pltpu.make_async_copy(shards[which], held[which], in_sem.at[which])

    def store(which):
        count = shards[which].shape[0]
        row = (here.z * 2 + here.core) * count
        there = pl.ds(pl.multiple_of(row, 16), count)
        return pltpu.make_async_copy(held[which], wholes[which].at[there], own_sem.at[which])

    def level(size):
        return [subset for subset in range(1, seq) if bin(subset).count("1") == size]

    shifts = range(1, chips)

    def begin(unit):
        for k in shifts:
            along(unit, k).start()
        turn(unit, 0).start()

    def arrive(unit):
        for k in shifts:
            along(unit, k).wait()
            for subset in level(1):
                spread(unit, k, subset).start()

    def pass_on(unit, size):
        for k in shifts:
            for subset in level(size):
                spread(unit, k, subset).wait()
            for subset in level(size + 1):
                spread(unit, k, subset).start()
            if size == bits:
                turn(unit, k).start()

    def finish(unit):
        for k in range(chips):
            turn(unit, k).wait()

    for which in range(weights):
        load(which).start()
    stages = [begin, arrive]
    for size in range(1, bits + 1):
        stages.append(lambda unit, size=size: pass_on(unit, size))
    stages.append(finish)
    begin(0)
    for now in range(len(units) + len(stages) - 2):
        for number, stage in enumerate(stages):
            unit = now - number + 1
            if 0 <= unit < len(units) and not (number == 0 and unit == 0):
                stage(unit)
        if now < weights:
            load(now).wait()
            store(now).start()
    for which in range(weights):
        if which >= len(units) + len(stages) - 2:
            load(which).wait()
            store(which).start()
    for which in range(weights):
        store(which).wait()


def gathered(shards, chips, bits, units):
    weights, seq, count = len(shards), 1 << bits, len(units)
    dma = pltpu.SemaphoreType.DMA
    return pl.pallas_call(
        functools.partial(gather_kernel, chips, bits, units, weights),
        out_shape=tuple(jax.ShapeDtypeStruct((2 * chips * one.shape[0], one.shape[1]), one.dtype) for one in shards),
        in_specs=[pl.BlockSpec(memory_space=pl.ANY)] * weights,
        out_specs=tuple(pl.BlockSpec(memory_space=pl.ANY) for _ in shards),
        scratch_shapes=[pltpu.VMEM(one.shape, one.dtype) for one in shards]
        + [
            dma((weights,)),
            dma((weights,)),
            dma((count, chips - 1)),
            dma((count, chips - 1)),
            dma((count, chips - 1, seq - 1)),
            dma((count, chips - 1, seq - 1)),
            dma((count, chips)),
            dma((count, chips)),
        ],
        compiler_params=pltpu.CompilerParams(
            collective_id=1, has_side_effects=True, vmem_limit_bytes=62 * 1024 * 1024
        ),
        cost_estimate=pl.CostEstimate(flops=0, bytes_accessed=900_000_000, transcendentals=0),
    )(*shards)


def parts_of(which, width, count):
    return tuple((which, i * (width // count), width // count) for i in range(count))


def sum_rows(terms):
    mine = lax.psum_scatter(terms, "batch", scatter_dimension=0, tiled=True)
    return lax.psum(mine, "seq").astype(F32)


def local(
    tokens,
    cotangent,
    segment_ids,
    positions,
    attn_gain,
    qkv_weight,
    out_weight,
    mlp_gain,
    gate_up_weight,
    down_weight,
):
    seq = lax.axis_size("seq")
    chips = lax.axis_size("batch") // 2
    bits = seq.bit_length() - 1
    s = lax.axis_index("seq")
    swap = [(i, i ^ 1) for i in range(seq)]
    model_width = tokens.shape[2]
    rows = tokens.shape[1]
    if rows * 2 != DOC_MAX:
        raise ValueError("token shard")
    share = H // KV
    kv_width = KV * HD
    scale_factor = HD ** (-0.5)
    ff_width = gate_up_weight.shape[1] // 2

    shards = (qkv_weight, out_weight, gate_up_weight, down_weight)
    cuts = (1, 1, 8, max(1, min(4, model_width // (seq * 128))))
    units = sum((parts_of(i, one.shape[1], n) for i, (one, n) in enumerate(zip(shards, cuts))), ())
    qkv_whole, out_whole, gate_up_whole, down_whole = gathered(shards, chips, bits, units)

    inputs = tokens[0].astype(F32)
    normed, inv_first = rms_parts(inputs, attn_gain)
    normed_low = normed.astype(BF16)
    projected = dot(normed_low, qkv_whole)

    row_start = s * rows
    own_segments = lax.dynamic_slice_in_dim(segment_ids[0], row_start, rows, 0)
    other = s ^ 1
    other_segments = lax.dynamic_slice_in_dim(segment_ids[0], other * rows, rows, 0)
    own_positions = lax.dynamic_slice_in_dim(positions[0], row_start, rows, 0)
    cosine, sine_part = rotary_tables(own_positions, HD)
    queries = projected[:, :model_width].astype(BF16).reshape(rows, H, HD)
    queries_rot = rotate(queries.astype(F32), cosine, sine_part).astype(BF16)
    queries_rot = queries_rot.reshape(rows, KV, share, HD)
    keys = projected[:, model_width : model_width + kv_width].astype(BF16).reshape(rows, KV, HD)
    keys_rot = rotate(keys.astype(F32), cosine, sine_part).astype(BF16).reshape(rows, kv_width)
    values = projected[:, model_width + kv_width :].astype(BF16)
    own_kv = jnp.concatenate([keys_rot, values], axis=1)
    other_kv = lax.ppermute(own_kv, "seq", swap)
    both_kv = jnp.concatenate([own_kv, other_kv], axis=0)
    all_keys = both_kv[:, :kv_width].reshape(2 * rows, KV, HD)
    all_values = both_kv[:, kv_width:].reshape(2 * rows, KV, HD)
    index = jnp.arange(rows, dtype=jnp.int32)
    allowed = jnp.concatenate(
        [
            (index[None, :] <= index[:, None]) & (own_segments[None, :] == own_segments[:, None]),
            (other < s) & (other_segments[None, :] == own_segments[:, None]),
        ],
        axis=1,
    )
    scores = (
        jnp.einsum("qgsd,kgd->gsqk", queries_rot, all_keys, preferred_element_type=F32)
        * scale_factor
    )
    masked = jnp.where(allowed[None, None], scores, -1e30)
    row_max = jnp.max(masked, axis=-1, keepdims=True)
    exps = jnp.exp(masked - row_max)
    probs = exps / jnp.sum(exps, axis=-1, keepdims=True)
    probs_low = probs.astype(BF16)
    attended = jnp.einsum("gsqk,kgd->qgsd", probs_low, all_values, preferred_element_type=F32)
    attended = attended.astype(BF16).reshape(rows, model_width)
    residual = inputs + dot(attended, out_whole)
    normed_mlp, inv_second = rms_parts(residual, mlp_gain)
    normed_mlp_low = normed_mlp.astype(BF16)
    gate_up = dot(normed_mlp_low, gate_up_whole)
    gate_part = gate_up[:, :ff_width]
    up_part = gate_up[:, ff_width:]
    sigmoid_gate = jax.nn.sigmoid(gate_part)
    hidden_low = (gate_part * sigmoid_gate * up_part).astype(BF16)
    output = (residual + dot(hidden_low, down_whole)).astype(BF16)

    grad_out = cotangent[0].astype(F32)
    grad_down = cotangent[0]
    down_terms = dot_tn(hidden_low, grad_down).astype(BF16)
    grad_hidden = dot_nt(grad_down, down_whole)
    grad_gate = grad_hidden * up_part * sigmoid_gate * (1.0 + gate_part * (1.0 - sigmoid_gate))
    grad_up = grad_hidden * gate_part * sigmoid_gate
    grad_gate_up = jnp.concatenate([grad_gate, grad_up], axis=1).astype(BF16)
    gate_up_terms = dot_tn(normed_mlp_low, grad_gate_up).astype(BF16)
    grad_normed_mlp = dot_nt(grad_gate_up, gate_up_whole)
    mlp_term = jnp.sum(grad_normed_mlp * residual * inv_second, axis=0)
    grad_resid = grad_out + norm_back(grad_normed_mlp, residual, inv_second, mlp_gain)
    grad_proj = grad_resid.astype(BF16)
    out_grad = sum_rows(dot_tn(attended, grad_proj).astype(BF16))
    grad_heads = dot_nt(grad_proj, out_whole)
    grad_heads = grad_heads.astype(BF16).reshape(rows, KV, share, HD)

    grad_probs = jnp.einsum("qgsd,kgd->gsqk", grad_heads, all_values, preferred_element_type=F32)
    inner_sum = jnp.sum(probs * grad_probs, axis=-1, keepdims=True)
    grad_scores = (probs * (grad_probs - inner_sum)).astype(BF16)
    grad_queries = (
        jnp.einsum("gsqk,kgd->qgsd", grad_scores, all_keys, preferred_element_type=F32)
        * scale_factor
    )
    grad_keys = (
        jnp.einsum("gsqk,qgsd->kgd", grad_scores, queries_rot, preferred_element_type=F32)
        * scale_factor
    )
    grad_values = jnp.einsum("gsqk,qgsd->kgd", probs_low, grad_heads, preferred_element_type=F32)
    grad_kv = jnp.concatenate(
        [grad_keys.reshape(2 * rows, kv_width), grad_values.reshape(2 * rows, kv_width)], axis=1
    )
    away = grad_kv[rows:].astype(BF16)
    arrived = lax.ppermute(away, "seq", swap)
    own_grad_kv = grad_kv[:rows] + arrived.astype(F32)
    back_queries = rotate(grad_queries.reshape(rows, H, HD), cosine, -sine_part)
    back_keys = rotate(own_grad_kv[:, :kv_width].reshape(rows, KV, HD), cosine, -sine_part)
    grad_qkv = jnp.concatenate(
        [
            back_queries.reshape(rows, model_width),
            back_keys.reshape(rows, kv_width),
            own_grad_kv[:, kv_width:],
        ],
        axis=1,
    ).astype(BF16)
    qkv_grad = sum_rows(dot_tn(normed_low, grad_qkv).astype(BF16))
    grad_normed = dot_nt(grad_qkv, qkv_whole)
    attn_term = jnp.sum(grad_normed * inputs * inv_first, axis=0)
    tokens_grad = (grad_resid + norm_back(grad_normed, inputs, inv_first, attn_gain)).astype(BF16)
    gains = jnp.concatenate([attn_term, mlp_term]).reshape(-1, 128)
    gate_up_grad, gains = reduced(gate_up_terms, gains, chips, bits, 11, 0)
    gains = gains.reshape(-1)
    if down_weight.shape[0] // seq % 16 == 0:
        down_grad, _ = reduced(down_terms, jnp.zeros((8, 128), F32), chips, bits, 8, 2)
    else:
        down_grad = sum_rows(down_terms)
    return (
        output[None],
        tokens_grad[None],
        gains[:model_width],
        qkv_grad,
        out_grad,
        gains[model_width:],
        gate_up_grad.astype(F32),
        down_grad.astype(F32),
    )


def solution(mesh):
    return jax.shard_map(
        local,
        mesh=mesh,
        in_specs=(
            P("batch", "seq", None),
            P("batch", "seq", None),
            P("batch", None),
            P("batch", None),
            P(),
            P("batch", None),
            P("batch", None),
            P(),
            P("batch", None),
            P("batch", None),
        ),
        out_specs=(
            P("batch", "seq", None),
            P("batch", "seq", None),
            P(),
            P("batch", None),
            P("batch", None),
            P(),
            P("batch", None),
            P("batch", None),
        ),
        check_vma=False,
    )
```

```python
import functools

import jax
import jax.numpy as jnp
from jax import lax
from jax.experimental import pallas as pl
from jax.experimental.pallas import tpu as pltpu
from jax.sharding import PartitionSpec as P

H = 32
KV = 4
HD = 64
DOC_MAX = 512
F32 = jnp.float32
BF16 = jnp.bfloat16


def rms_parts(values, gain_vector):
    inv_rms = lax.rsqrt(jnp.mean(values * values, axis=-1, keepdims=True) + 1e-05)
    return (values * inv_rms * gain_vector, inv_rms)


def norm_back(grad_normed, values, inv_rms, gain_vector):
    weighted = grad_normed * gain_vector
    inner_sum = jnp.mean(weighted * values, axis=-1, keepdims=True)
    return inv_rms * weighted - values * (inv_rms * inv_rms * inv_rms) * inner_sum


def rotary_tables(seq_positions, head_dim):
    half_dim = head_dim // 2
    frequency = 10000.0 ** (-jnp.arange(half_dim, dtype=F32) * 2.0 / head_dim)
    angles = seq_positions.astype(F32)[:, None] * frequency[None, :]
    return (jnp.cos(angles)[:, None, :], jnp.sin(angles)[:, None, :])


def rotate(values, cosine, sine_part):
    half_dim = values.shape[-1] // 2
    first_half = values[..., :half_dim]
    second_half = values[..., half_dim:]
    return jnp.concatenate(
        [
            first_half * cosine - second_half * sine_part,
            second_half * cosine + first_half * sine_part,
        ],
        axis=-1,
    )


def dot(left, right):
    return jnp.dot(left, right, preferred_element_type=F32)


def dot_nt(left, right):
    return lax.dot_general(left, right, (((1,), (1,)), ((), ())), preferred_element_type=F32)


def dot_tn(left, right):
    return lax.dot_general(left, right, (((0,), (0,)), ((), ())), preferred_element_type=F32)


class Place:
    def __init__(self, chips, bits):
        self.chips, self.bits = chips, bits
        self.s = lax.axis_index("seq")
        place = lax.axis_index("batch")
        self.z, self.core = place // 2, place % 2
        reverse = 0
        for bit in range(bits):
            reverse = reverse + ((self.s // (1 << bit)) % 2) * (1 << (bits - 1 - bit))
        self.part = reverse + self.core * (self.s - reverse)

    def sibling(self):
        return {"batch": self.z * 2 + 1 - self.core}

    def chip(self, shift):
        return {"batch": ((self.z + shift) % self.chips) * 2 + self.core}

    def partner(self, step):
        first, second = 1 << step, 1 << (self.bits - 1 - step)
        mask = first + self.core * (second - first)
        return {"seq": self.s + mask * (1 - 2 * ((self.s // mask) % 2))}

    def fellows(self):
        found = [self.sibling()] + [self.partner(step) for step in range(self.bits)]
        step = 1
        while step < self.chips:
            found.append({"batch": (self.z + step * (1 - 2 * ((self.z // step) % 2))) * 2 + self.core})
            step *= 2
        return found

    def bit(self, step):
        return (self.part // (1 << (self.bits - 1 - step))) % 2

    def part_of(self, subset):
        part = self.part
        for step in range(self.bits):
            if subset >> step & 1:
                weight = 1 << (self.bits - 1 - step)
                part = part + weight * (1 - 2 * self.bit(step))
        return part


def reduce_kernel(chips, bits, count, terms, small, out, arrived, small_out, *scratch):
    halves = scratch[:bits]
    own, got, along, final = scratch[bits : bits + 4]
    (own_sem, got_sem, core_out, core_in, half_out, half_in, along_out, along_in, spread_out, spread_in, local_sem) = (
        scratch[bits + 4 : -4]
    )
    small_sum, small_got, small_send, small_recv = scratch[-4:]
    here = Place(chips, bits)
    rows, width = own.shape[2], own.shape[3]
    piece = rows >> bits
    slots = own.shape[0]
    seq = 1 << bits

    barrier = pltpu.get_barrier_semaphore()
    peers = [here.sibling()] + [here.partner(i) for i in range(bits)] + [here.chip(k) for k in range(1, chips)]
    fellows = here.fellows()
    for peer in peers:
        pl.semaphore_signal(barrier, inc=1, device_id=peer, device_id_type=pl.DeviceIdType.MESH)
    pl.semaphore_wait(barrier, len(peers))

    def columns(j):
        return pl.ds(pl.multiple_of(j * width, 128), width)

    def core_copy(j):
        return pltpu.make_async_remote_copy(
            src_ref=terms.at[:, 1 - here.core, :, columns(j)],
            dst_ref=arrived.at[j],
            send_sem=core_out.at[j],
            recv_sem=core_in.at[j],
            device_id=here.sibling(),
            device_id_type=pl.DeviceIdType.MESH,
        )

    def own_load(j):
        return pltpu.make_async_copy(terms.at[:, here.core, :, columns(j)], own.at[j % slots], own_sem.at[j])

    def got_load(j):
        return pltpu.make_async_copy(arrived.at[j], got.at[j % 2], got_sem.at[j])

    def offset(step):
        total = 0
        for i in range(step):
            total = total + here.bit(i) * (rows >> (i + 1))
        return total

    def half_copy(j, step):
        half = rows >> (step + 1)
        first = pl.multiple_of(offset(step) + (1 - here.bit(step)) * half, piece)
        return pltpu.make_async_remote_copy(
            src_ref=own.at[j % slots, :, pl.ds(first, half), :],
            dst_ref=halves[step].at[j],
            send_sem=half_out.at[j, step],
            recv_sem=half_in.at[j, step],
            device_id=here.partner(step),
            device_id_type=pl.DeviceIdType.MESH,
        )

    def along_copy(j, k):
        first = pl.multiple_of(offset(bits), piece)
        return pltpu.make_async_remote_copy(
            src_ref=own.at[j % slots, (here.z + k) % chips, pl.ds(first, piece), :],
            dst_ref=along.at[j, k - 1],
            send_sem=along_out.at[j, k - 1],
            recv_sem=along_in.at[j, k - 1],
            device_id=here.chip(k),
            device_id_type=pl.DeviceIdType.MESH,
        )

    def place_of(j, subset):
        return out.at[pl.ds(pl.multiple_of(here.part_of(subset) * piece, piece), piece), columns(j)]

    def spread_copy(j, subset):
        last = subset.bit_length() - 1
        parent = subset ^ (1 << last)
        return pltpu.make_async_remote_copy(
            src_ref=final.at[j] if parent == 0 else place_of(j, parent),
            dst_ref=place_of(j, parent),
            send_sem=spread_out.at[j, subset - 1],
            recv_sem=spread_in.at[j, subset - 1],
            device_id=here.partner(last),
            device_id_type=pl.DeviceIdType.MESH,
        )

    def local_copy(j):
        return pltpu.make_async_copy(final.at[j], place_of(j, 0), local_sem.at[j])

    def level(size):
        return [subset for subset in range(1, seq) if bin(subset).count("1") == size]

    def fresh(j):
        core_copy(j).start()

    def loads(j):
        core_copy(j).wait()
        own_load(j).start()
        got_load(j).start()

    def first_sum(j):
        own_load(j).wait()
        got_load(j).wait()
        block = 32 if rows % 32 == 0 else 16
        blocks = rows // block
        slot = j % slots

        def body(index, carry):
            z = index // blocks
            span = pl.ds(pl.multiple_of((index % blocks) * block, block), block)
            own[slot, z, span, :] = (
                own[slot, z, span, :].astype(F32) + got[j % 2, z, span, :].astype(F32)
            ).astype(BF16)
            return carry

        lax.fori_loop(0, chips * blocks, body, 0)

    def half_sum(j, step):
        half_copy(j, step).wait()
        half = rows >> (step + 1)
        block = 32 if half % 32 == 0 else 16
        blocks = half // block
        slot = j % slots
        start = offset(step + 1)

        def body(index, carry):
            z = index // blocks
            first = (index % blocks) * block
            there = pl.ds(pl.multiple_of(first, block), block)
            span = pl.ds(pl.multiple_of(start + first, block), block)
            own[slot, z, span, :] = (
                own[slot, z, span, :].astype(F32) + halves[step][j, z, there, :].astype(F32)
            ).astype(BF16)
            return carry

        lax.fori_loop(0, chips * blocks, body, 0)

    def send_along(j):
        for k in range(1, chips):
            along_copy(j, k).start()

    def last_sum(j):
        for k in range(1, chips):
            along_copy(j, k).wait()
        block = 16
        slot = j % slots
        start = offset(bits)

        def body(index, carry):
            first = index * block
            there = pl.ds(pl.multiple_of(first, block), block)
            total = own[slot, here.z, pl.ds(pl.multiple_of(start + first, block), block), :].astype(F32)
            for k in range(chips - 1):
                total = total + along[j, k, there, :].astype(F32)
            final[j, there, :] = total.astype(BF16)
            return carry

        lax.fori_loop(0, piece // block, body, 0)
        local_copy(j).start()
        for subset in level(1):
            spread_copy(j, subset).start()

    def pass_on(j, size):
        for subset in level(size):
            spread_copy(j, subset).wait()
        for subset in level(size + 1):
            spread_copy(j, subset).start()

    def small_copy(step):
        return pltpu.make_async_remote_copy(
            src_ref=small_sum.at[step],
            dst_ref=small_got.at[step],
            send_sem=small_send.at[step],
            recv_sem=small_recv.at[step],
            device_id=fellows[step],
            device_id_type=pl.DeviceIdType.MESH,
        )

    def small_step(step):
        if step:
            small_copy(step - 1).wait()
            small_sum[step] = small_sum[step - 1] + small_got[step - 1]
        if step < len(fellows):
            small_copy(step).start()
        else:
            small_out[...] = small_sum[step]

    stages = [fresh, loads, first_sum, lambda j: half_copy(j, 0).start()]
    for step in range(bits):

        def stage(j, step=step):
            half_sum(j, step)
            if step + 1 < bits:
                half_copy(j, step + 1).start()
            else:
                send_along(j)

        stages.append(stage)
    stages.append(last_sum)
    for size in range(1, bits + 1):
        stages.append(lambda j, size=size: pass_on(j, size))
    stages.append(lambda j: local_copy(j).wait())
    order = list(range(3, len(stages))) + [2, 1, 0]

    def round_of(now, carry):
        for step in range(len(fellows) + 1):

            @pl.when(now == step)
            def _(step=step):
                small_step(step)

        for number in order:
            chunk = now - number

            @pl.when((chunk >= 0) & (chunk < count))
            def _(number=number, chunk=chunk):
                stages[number](chunk)

        return carry

    small_sum[0] = small[...]
    lax.fori_loop(0, count + len(stages) - 1, round_of, 0)


def reduced(terms, small, chips, bits, count, number):
    rows, width = terms.shape[0] // (2 * chips), terms.shape[1]
    seq, wide = 1 << bits, width // count
    piece = rows // seq
    slots = bits + 5
    dma = pltpu.SemaphoreType.DMA
    steps = 1 + bits + (chips - 1).bit_length()
    out, _, small_out = pl.pallas_call(
        functools.partial(reduce_kernel, chips, bits, count),
        out_shape=(
            jax.ShapeDtypeStruct((rows, width), BF16),
            jax.ShapeDtypeStruct((count, chips, rows, wide), BF16),
            jax.ShapeDtypeStruct(small.shape, F32),
        ),
        in_specs=[pl.BlockSpec(memory_space=pl.ANY), pl.BlockSpec(memory_space=pltpu.VMEM)],
        out_specs=(
            pl.BlockSpec(memory_space=pl.ANY),
            pl.BlockSpec(memory_space=pl.ANY),
            pl.BlockSpec(memory_space=pltpu.VMEM),
        ),
        scratch_shapes=[pltpu.VMEM((count, chips, rows >> (step + 1), wide), BF16) for step in range(bits)]
        + [
            pltpu.VMEM((slots, chips, rows, wide), BF16),
            pltpu.VMEM((2, chips, rows, wide), BF16),
            pltpu.VMEM((count, chips - 1, piece, wide), BF16),
            pltpu.VMEM((count, piece, wide), BF16),
            dma((count,)),
            dma((count,)),
            dma((count,)),
            dma((count,)),
            dma((count, bits)),
            dma((count, bits)),
            dma((count, chips - 1)),
            dma((count, chips - 1)),
            dma((count, seq - 1)),
            dma((count, seq - 1)),
            dma((count,)),
            pltpu.VMEM((steps + 1,) + small.shape, F32),
            pltpu.VMEM((steps,) + small.shape, F32),
            dma((steps,)),
            dma((steps,)),
        ],
        compiler_params=pltpu.CompilerParams(
            collective_id=number, has_side_effects=True, vmem_limit_bytes=62 * 1024 * 1024
        ),
        cost_estimate=pl.CostEstimate(flops=0, bytes_accessed=800_000_000, transcendentals=0),
    )(terms.reshape(chips, 2, rows, width), small)
    return out, small_out


def gather_kernel(chips, bits, units, weights, ahead, *refs):
    shards, wholes = refs[:weights], refs[weights : 2 * weights]
    held = refs[2 * weights : 3 * weights]
    (in_sem, own_sem, along_out, along_in, spread_out, spread_in, turn_out, turn_in) = refs[3 * weights :]
    here = Place(chips, bits)
    seq = 1 << bits

    barrier = pltpu.get_barrier_semaphore()
    peers = [here.sibling()] + [here.partner(i) for i in range(bits)] + [here.chip(k) for k in range(1, chips)]
    for peer in peers:
        pl.semaphore_signal(barrier, inc=1, device_id=peer, device_id_type=pl.DeviceIdType.MESH)
    pl.semaphore_wait(barrier, len(peers))

    def rows_of(unit, shift):
        which, first, width = units[unit]
        count = shards[which].shape[0]
        row = (((here.z - shift) % chips) * 2 + here.core) * count
        return which, row, count, first, width

    def piece_of(unit, shift, subset):
        which, row, count, first, width = rows_of(unit, shift)
        part = here.part_of(subset)
        if (count // seq) % 16 == 0:
            size = count // seq
            return which, pl.ds(pl.multiple_of(row + part * size, 16), size), pl.ds(first, width)
        size = width // seq
        return which, pl.ds(pl.multiple_of(row, 16), count), pl.ds(pl.multiple_of(first + part * size, 128), size)

    def remote(source, target, sems, index, device):
        return pltpu.make_async_remote_copy(
            src_ref=source,
            dst_ref=target,
            send_sem=sems[0].at[index],
            recv_sem=sems[1].at[index],
            device_id=device,
            device_id_type=pl.DeviceIdType.MESH,
        )

    def along(unit, k):
        which, row, count, first, width = rows_of(unit, 0)
        _, there, columns = piece_of(unit, 0, 0)
        part = here.part
        if (count // seq) % 16 == 0:
            size = count // seq
            source = shards[which].at[pl.ds(pl.multiple_of(part * size, 16), size), columns]
        else:
            source = shards[which].at[:, columns]
        return remote(source, wholes[which].at[there, columns], (along_out, along_in), (unit, k - 1), here.chip(k))

    def spread(unit, k, subset):
        last = subset.bit_length() - 1
        which, there, columns = piece_of(unit, k, subset ^ (1 << last))
        region = wholes[which].at[there, columns]
        return remote(region, region, (spread_out, spread_in), (unit, k - 1, subset - 1), here.partner(last))

    def turn(unit, k):
        which, row, count, first, width = rows_of(unit, k)
        there = pl.ds(pl.multiple_of(row, 16), count)
        region = wholes[which].at[there, pl.ds(first, width)]
        source = region if k else shards[which].at[:, pl.ds(first, width)]
        return remote(source, region, (turn_out, turn_in), (unit, k), here.sibling())

    def load(which):
        return pltpu.make_async_copy(shards[which], held[which], in_sem.at[which])

    def store(which):
        count = shards[which].shape[0]
        row = (here.z * 2 + here.core) * count
        there = pl.ds(pl.multiple_of(row, 16), count)
        return pltpu.make_async_copy(held[which], wholes[which].at[there], own_sem.at[which])

    def level(size):
        return [subset for subset in range(1, seq) if bin(subset).count("1") == size]

    shifts = range(1, chips)

    def begin(unit):
        for k in shifts:
            along(unit, k).start()
        turn(unit, 0).start()

    def arrive(unit):
        for k in shifts:
            along(unit, k).wait()
            for subset in level(1):
                spread(unit, k, subset).start()

    def pass_on(unit, size):
        for k in shifts:
            for subset in level(size):
                spread(unit, k, subset).wait()
            for subset in level(size + 1):
                spread(unit, k, subset).start()
            if size == bits:
                turn(unit, k).start()

    def finish(unit):
        for k in range(chips):
            turn(unit, k).wait()

    for which in range(weights):
        load(which).start()
    stages = [arrive]
    for size in range(1, bits + 1):
        stages.append(lambda unit, size=size: pass_on(unit, size))
    stages.append(finish)
    for unit in range(min(ahead, len(units))):
        begin(unit)
    for now in range(len(units) + len(stages) - 1):
        if now + ahead < len(units):
            begin(now + ahead)
        for number, stage in enumerate(stages):
            unit = now - number
            if 0 <= unit < len(units):
                stage(unit)
        if now < weights:
            load(now).wait()
            store(now).start()
    for which in range(weights):
        if which >= len(units) + len(stages) - 1:
            load(which).wait()
            store(which).start()
    for which in range(weights):
        store(which).wait()


def gathered(shards, chips, bits, units, ahead):
    weights, seq, count = len(shards), 1 << bits, len(units)
    dma = pltpu.SemaphoreType.DMA
    return pl.pallas_call(
        functools.partial(gather_kernel, chips, bits, units, weights, ahead),
        out_shape=tuple(jax.ShapeDtypeStruct((2 * chips * one.shape[0], one.shape[1]), one.dtype) for one in shards),
        in_specs=[pl.BlockSpec(memory_space=pl.ANY)] * weights,
        out_specs=tuple(pl.BlockSpec(memory_space=pl.ANY) for _ in shards),
        scratch_shapes=[pltpu.VMEM(one.shape, one.dtype) for one in shards]
        + [
            dma((weights,)),
            dma((weights,)),
            dma((count, chips - 1)),
            dma((count, chips - 1)),
            dma((count, chips - 1, seq - 1)),
            dma((count, chips - 1, seq - 1)),
            dma((count, chips)),
            dma((count, chips)),
        ],
        compiler_params=pltpu.CompilerParams(
            collective_id=1, has_side_effects=True, vmem_limit_bytes=62 * 1024 * 1024
        ),
        cost_estimate=pl.CostEstimate(flops=0, bytes_accessed=900_000_000, transcendentals=0),
    )(*shards)


def parts_of(which, width, count):
    return tuple((which, i * (width // count), width // count) for i in range(count))


def scatter_rows(terms):
    return lax.psum_scatter(terms, "batch", scatter_dimension=0, tiled=True)


def local(
    tokens,
    cotangent,
    segment_ids,
    positions,
    attn_gain,
    qkv_weight,
    out_weight,
    mlp_gain,
    gate_up_weight,
    down_weight,
):
    seq = lax.axis_size("seq")
    chips = lax.axis_size("batch") // 2
    bits = seq.bit_length() - 1
    s = lax.axis_index("seq")
    swap = [(i, i ^ 1) for i in range(seq)]
    model_width = tokens.shape[2]
    rows = tokens.shape[1]
    if rows * 2 != DOC_MAX:
        raise ValueError("token shard")
    share = H // KV
    kv_width = KV * HD
    scale_factor = HD ** (-0.5)
    ff_width = gate_up_weight.shape[1] // 2

    shards = (qkv_weight, out_weight, gate_up_weight, down_weight)
    cuts = (2, 2, 8, max(1, min(4, model_width // (seq * 128))))
    units = sum((parts_of(i, one.shape[1], n) for i, (one, n) in enumerate(zip(shards, cuts))), ())
    qkv_whole, out_whole, gate_up_whole, down_whole = gathered(shards, chips, bits, units, 3)

    inputs = tokens[0].astype(F32)
    normed, inv_first = rms_parts(inputs, attn_gain)
    normed_low = normed.astype(BF16)
    projected = dot(normed_low, qkv_whole)

    row_start = s * rows
    own_segments = lax.dynamic_slice_in_dim(segment_ids[0], row_start, rows, 0)
    other = s ^ 1
    other_segments = lax.dynamic_slice_in_dim(segment_ids[0], other * rows, rows, 0)
    own_positions = lax.dynamic_slice_in_dim(positions[0], row_start, rows, 0)
    cosine, sine_part = rotary_tables(own_positions, HD)
    queries = projected[:, :model_width].astype(BF16).reshape(rows, H, HD)
    queries_rot = rotate(queries.astype(F32), cosine, sine_part).astype(BF16)
    queries_rot = queries_rot.reshape(rows, KV, share, HD)
    keys = projected[:, model_width : model_width + kv_width].astype(BF16).reshape(rows, KV, HD)
    keys_rot = rotate(keys.astype(F32), cosine, sine_part).astype(BF16).reshape(rows, kv_width)
    values = projected[:, model_width + kv_width :].astype(BF16)
    own_kv = jnp.concatenate([keys_rot, values], axis=1)
    other_kv = lax.ppermute(own_kv, "seq", swap)
    both_kv = jnp.concatenate([own_kv, other_kv], axis=0)
    all_keys = both_kv[:, :kv_width].reshape(2 * rows, KV, HD)
    all_values = both_kv[:, kv_width:].reshape(2 * rows, KV, HD)
    index = jnp.arange(rows, dtype=jnp.int32)
    allowed = jnp.concatenate(
        [
            (index[None, :] <= index[:, None]) & (own_segments[None, :] == own_segments[:, None]),
            (other < s) & (other_segments[None, :] == own_segments[:, None]),
        ],
        axis=1,
    )
    scores = (
        jnp.einsum("qgsd,kgd->gsqk", queries_rot, all_keys, preferred_element_type=F32)
        * scale_factor
    )
    masked = jnp.where(allowed[None, None], scores, -1e30)
    row_max = jnp.max(masked, axis=-1, keepdims=True)
    exps = jnp.exp(masked - row_max)
    probs = exps / jnp.sum(exps, axis=-1, keepdims=True)
    probs_low = probs.astype(BF16)
    attended = jnp.einsum("gsqk,kgd->qgsd", probs_low, all_values, preferred_element_type=F32)
    attended = attended.astype(BF16).reshape(rows, model_width)
    residual = inputs + dot(attended, out_whole)
    normed_mlp, inv_second = rms_parts(residual, mlp_gain)
    normed_mlp_low = normed_mlp.astype(BF16)
    gate_up = dot(normed_mlp_low, gate_up_whole)
    gate_part = gate_up[:, :ff_width]
    up_part = gate_up[:, ff_width:]
    sigmoid_gate = jax.nn.sigmoid(gate_part)
    hidden_low = (gate_part * sigmoid_gate * up_part).astype(BF16)
    output = (residual + dot(hidden_low, down_whole)).astype(BF16)

    grad_out = cotangent[0].astype(F32)
    grad_down = cotangent[0]
    early = model_width * 4 // 8
    early_terms = dot_tn(hidden_low, grad_down[:, :early]).astype(BF16)
    early_terms, grad_down = lax.optimization_barrier((early_terms, grad_down))
    down_early = scatter_rows(early_terms)
    down_terms = dot_tn(hidden_low, grad_down[:, early:]).astype(BF16)
    grad_hidden = dot_nt(grad_down, down_whole)
    grad_gate = grad_hidden * up_part * sigmoid_gate * (1.0 + gate_part * (1.0 - sigmoid_gate))
    grad_up = grad_hidden * gate_part * sigmoid_gate
    grad_gate_up = jnp.concatenate([grad_gate, grad_up], axis=1).astype(BF16)
    gate_up_terms = dot_tn(normed_mlp_low, grad_gate_up).astype(BF16)
    grad_normed_mlp = dot_nt(grad_gate_up, gate_up_whole)
    mlp_term = jnp.sum(grad_normed_mlp * residual * inv_second, axis=0)
    grad_resid = grad_out + norm_back(grad_normed_mlp, residual, inv_second, mlp_gain)
    grad_proj = grad_resid.astype(BF16)
    out_part = scatter_rows(dot_tn(attended, grad_proj).astype(BF16))
    grad_heads = dot_nt(grad_proj, out_whole)
    grad_heads = grad_heads.astype(BF16).reshape(rows, KV, share, HD)

    grad_probs = jnp.einsum("qgsd,kgd->gsqk", grad_heads, all_values, preferred_element_type=F32)
    inner_sum = jnp.sum(probs * grad_probs, axis=-1, keepdims=True)
    grad_scores = (probs * (grad_probs - inner_sum)).astype(BF16)
    grad_queries = (
        jnp.einsum("gsqk,kgd->qgsd", grad_scores, all_keys, preferred_element_type=F32)
        * scale_factor
    )
    grad_keys = (
        jnp.einsum("gsqk,qgsd->kgd", grad_scores, queries_rot, preferred_element_type=F32)
        * scale_factor
    )
    grad_values = jnp.einsum("gsqk,qgsd->kgd", probs_low, grad_heads, preferred_element_type=F32)
    grad_kv = jnp.concatenate(
        [grad_keys.reshape(2 * rows, kv_width), grad_values.reshape(2 * rows, kv_width)], axis=1
    )
    away = grad_kv[rows:].astype(BF16)
    arrived = lax.ppermute(away, "seq", swap)
    own_grad_kv = grad_kv[:rows] + arrived.astype(F32)
    back_queries = rotate(grad_queries.reshape(rows, H, HD), cosine, -sine_part)
    back_keys = rotate(own_grad_kv[:, :kv_width].reshape(rows, KV, HD), cosine, -sine_part)
    grad_qkv = jnp.concatenate(
        [
            back_queries.reshape(rows, model_width),
            back_keys.reshape(rows, kv_width),
            own_grad_kv[:, kv_width:],
        ],
        axis=1,
    ).astype(BF16)
    qkv_terms, down_early = lax.optimization_barrier((dot_tn(normed_low, grad_qkv).astype(BF16), down_early))
    qkv_part = scatter_rows(qkv_terms)
    grad_normed = dot_nt(grad_qkv, qkv_whole)
    attn_term = jnp.sum(grad_normed * inputs * inv_first, axis=0)
    tokens_grad = (grad_resid + norm_back(grad_normed, inputs, inv_first, attn_gain)).astype(BF16)
    gains = jnp.concatenate([attn_term, mlp_term]).reshape(-1, 128)
    gate_up_grad, gains = reduced(gate_up_terms, gains, chips, bits, 11, 0)
    gains = gains.reshape(-1)
    gate_up_grad, down_early, out_part, qkv_part, down_terms = lax.optimization_barrier(
        (gate_up_grad, down_early, out_part, qkv_part, down_terms)
    )
    if down_weight.shape[0] // seq % 16 == 0:
        down_late, _ = reduced(down_terms, jnp.zeros((8, 128), F32), chips, bits, 4, 2)
    else:
        down_late = lax.psum(scatter_rows(down_terms), "seq")
    down_early, out_grad, qkv_grad = lax.psum((down_early, out_part, qkv_part), "seq")
    down_grad = jnp.concatenate([down_early, down_late], axis=1)
    return (
        output[None],
        tokens_grad[None],
        gains[:model_width],
        qkv_grad.astype(F32),
        out_grad.astype(F32),
        gains[model_width:],
        gate_up_grad.astype(F32),
        down_grad.astype(F32),
    )


def solution(mesh):
    return jax.shard_map(
        local,
        mesh=mesh,
        in_specs=(
            P("batch", "seq", None),
            P("batch", "seq", None),
            P("batch", None),
            P("batch", None),
            P(),
            P("batch", None),
            P("batch", None),
            P(),
            P("batch", None),
            P("batch", None),
        ),
        out_specs=(
            P("batch", "seq", None),
            P("batch", "seq", None),
            P(),
            P("batch", None),
            P("batch", None),
            P(),
            P("batch", None),
            P("batch", None),
        ),
        check_vma=False,
    )
```

```python
import functools

import jax
import jax.numpy as jnp
from jax import lax
from jax.experimental import pallas as pl
from jax.experimental.pallas import tpu as pltpu
from jax.sharding import PartitionSpec as P

H = 32
KV = 4
HD = 64
DOC_MAX = 512
F32 = jnp.float32
BF16 = jnp.bfloat16


def rms_parts(values, gain_vector):
    inv_rms = lax.rsqrt(jnp.mean(values * values, axis=-1, keepdims=True) + 1e-05)
    return (values * inv_rms * gain_vector, inv_rms)


def norm_back(grad_normed, values, inv_rms, gain_vector):
    weighted = grad_normed * gain_vector
    inner_sum = jnp.mean(weighted * values, axis=-1, keepdims=True)
    return inv_rms * weighted - values * (inv_rms * inv_rms * inv_rms) * inner_sum


def rotary_tables(seq_positions, head_dim):
    half_dim = head_dim // 2
    frequency = 10000.0 ** (-jnp.arange(half_dim, dtype=F32) * 2.0 / head_dim)
    angles = seq_positions.astype(F32)[:, None] * frequency[None, :]
    return (jnp.cos(angles)[:, None, :], jnp.sin(angles)[:, None, :])


def rotate(values, cosine, sine_part):
    half_dim = values.shape[-1] // 2
    first_half = values[..., :half_dim]
    second_half = values[..., half_dim:]
    return jnp.concatenate(
        [
            first_half * cosine - second_half * sine_part,
            second_half * cosine + first_half * sine_part,
        ],
        axis=-1,
    )


def dot(left, right):
    return jnp.dot(left, right, preferred_element_type=F32)


def dot_nt(left, right):
    return lax.dot_general(left, right, (((1,), (1,)), ((), ())), preferred_element_type=F32)


def dot_tn(left, right):
    return lax.dot_general(left, right, (((0,), (0,)), ((), ())), preferred_element_type=F32)


class Place:
    def __init__(self, chips, bits):
        self.chips, self.bits = chips, bits
        self.s = lax.axis_index("seq")
        place = lax.axis_index("batch")
        self.z, self.core = place // 2, place % 2
        reverse = 0
        for bit in range(bits):
            reverse = reverse + ((self.s // (1 << bit)) % 2) * (1 << (bits - 1 - bit))
        self.part = reverse + self.core * (self.s - reverse)

    def sibling(self):
        return {"batch": self.z * 2 + 1 - self.core}

    def chip(self, shift):
        return {"batch": ((self.z + shift) % self.chips) * 2 + self.core}

    def partner(self, step):
        first, second = 1 << step, 1 << (self.bits - 1 - step)
        mask = first + self.core * (second - first)
        return {"seq": self.s + mask * (1 - 2 * ((self.s // mask) % 2))}

    def fellows(self):
        found = [self.sibling()] + [self.partner(step) for step in range(self.bits)]
        step = 1
        while step < self.chips:
            found.append({"batch": (self.z + step * (1 - 2 * ((self.z // step) % 2))) * 2 + self.core})
            step *= 2
        return found

    def bit(self, step):
        return (self.part // (1 << (self.bits - 1 - step))) % 2

    def part_of(self, subset):
        part = self.part
        for step in range(self.bits):
            if subset >> step & 1:
                weight = 1 << (self.bits - 1 - step)
                part = part + weight * (1 - 2 * self.bit(step))
        return part


def reduce_kernel(chips, bits, count, terms, small, out, arrived, small_out, *scratch):
    halves = scratch[:bits]
    own, got, along, final = scratch[bits : bits + 4]
    (own_sem, got_sem, core_out, core_in, half_out, half_in, along_out, along_in, spread_out, spread_in, local_sem) = (
        scratch[bits + 4 : -4]
    )
    small_sum, small_got, small_send, small_recv = scratch[-4:]
    here = Place(chips, bits)
    rows, width = own.shape[2], own.shape[3]
    piece = rows >> bits
    slots = own.shape[0]
    seq = 1 << bits

    barrier = pltpu.get_barrier_semaphore()
    peers = [here.sibling()] + [here.partner(i) for i in range(bits)] + [here.chip(k) for k in range(1, chips)]
    fellows = here.fellows()
    for peer in peers:
        pl.semaphore_signal(barrier, inc=1, device_id=peer, device_id_type=pl.DeviceIdType.MESH)
    pl.semaphore_wait(barrier, len(peers))

    def columns(j):
        return pl.ds(pl.multiple_of(j * width, 128), width)

    def core_copy(j):
        return pltpu.make_async_remote_copy(
            src_ref=terms.at[:, 1 - here.core, :, columns(j)],
            dst_ref=arrived.at[j],
            send_sem=core_out.at[j],
            recv_sem=core_in.at[j],
            device_id=here.sibling(),
            device_id_type=pl.DeviceIdType.MESH,
        )

    def own_load(j):
        return pltpu.make_async_copy(terms.at[:, here.core, :, columns(j)], own.at[j % slots], own_sem.at[j])

    def got_load(j):
        return pltpu.make_async_copy(arrived.at[j], got.at[j % 2], got_sem.at[j])

    def offset(step):
        total = 0
        for i in range(step):
            total = total + here.bit(i) * (rows >> (i + 1))
        return total

    def half_copy(j, step):
        half = rows >> (step + 1)
        first = pl.multiple_of(offset(step) + (1 - here.bit(step)) * half, piece)
        return pltpu.make_async_remote_copy(
            src_ref=own.at[j % slots, :, pl.ds(first, half), :],
            dst_ref=halves[step].at[j],
            send_sem=half_out.at[j, step],
            recv_sem=half_in.at[j, step],
            device_id=here.partner(step),
            device_id_type=pl.DeviceIdType.MESH,
        )

    def along_copy(j, k):
        first = pl.multiple_of(offset(bits), piece)
        return pltpu.make_async_remote_copy(
            src_ref=own.at[j % slots, (here.z + k) % chips, pl.ds(first, piece), :],
            dst_ref=along.at[j, k - 1],
            send_sem=along_out.at[j, k - 1],
            recv_sem=along_in.at[j, k - 1],
            device_id=here.chip(k),
            device_id_type=pl.DeviceIdType.MESH,
        )

    def place_of(j, subset):
        return out.at[pl.ds(pl.multiple_of(here.part_of(subset) * piece, piece), piece), columns(j)]

    def spread_copy(j, subset):
        last = subset.bit_length() - 1
        parent = subset ^ (1 << last)
        return pltpu.make_async_remote_copy(
            src_ref=final.at[j] if parent == 0 else place_of(j, parent),
            dst_ref=place_of(j, parent),
            send_sem=spread_out.at[j, subset - 1],
            recv_sem=spread_in.at[j, subset - 1],
            device_id=here.partner(last),
            device_id_type=pl.DeviceIdType.MESH,
        )

    def local_copy(j):
        return pltpu.make_async_copy(final.at[j], place_of(j, 0), local_sem.at[j])

    def level(size):
        return [subset for subset in range(1, seq) if bin(subset).count("1") == size]

    def fresh(j):
        core_copy(j).start()

    def loads(j):
        core_copy(j).wait()
        own_load(j).start()
        got_load(j).start()

    def first_sum(j):
        own_load(j).wait()
        got_load(j).wait()
        block = 32 if rows % 32 == 0 else 16
        blocks = rows // block
        slot = j % slots

        def body(index, carry):
            z = index // blocks
            span = pl.ds(pl.multiple_of((index % blocks) * block, block), block)
            own[slot, z, span, :] = (
                own[slot, z, span, :].astype(F32) + got[j % 2, z, span, :].astype(F32)
            ).astype(BF16)
            return carry

        lax.fori_loop(0, chips * blocks, body, 0)

    def half_sum(j, step):
        half_copy(j, step).wait()
        half = rows >> (step + 1)
        block = 32 if half % 32 == 0 else 16
        blocks = half // block
        slot = j % slots
        start = offset(step + 1)

        def body(index, carry):
            z = index // blocks
            first = (index % blocks) * block
            there = pl.ds(pl.multiple_of(first, block), block)
            span = pl.ds(pl.multiple_of(start + first, block), block)
            own[slot, z, span, :] = (
                own[slot, z, span, :].astype(F32) + halves[step][j, z, there, :].astype(F32)
            ).astype(BF16)
            return carry

        lax.fori_loop(0, chips * blocks, body, 0)

    def send_along(j):
        for k in range(1, chips):
            along_copy(j, k).start()

    def last_sum(j):
        for k in range(1, chips):
            along_copy(j, k).wait()
        block = 16
        slot = j % slots
        start = offset(bits)

        def body(index, carry):
            first = index * block
            there = pl.ds(pl.multiple_of(first, block), block)
            total = own[slot, here.z, pl.ds(pl.multiple_of(start + first, block), block), :].astype(F32)
            for k in range(chips - 1):
                total = total + along[j, k, there, :].astype(F32)
            final[j, there, :] = total.astype(BF16)
            return carry

        lax.fori_loop(0, piece // block, body, 0)
        local_copy(j).start()
        for subset in level(1):
            spread_copy(j, subset).start()

    def pass_on(j, size):
        for subset in level(size):
            spread_copy(j, subset).wait()
        for subset in level(size + 1):
            spread_copy(j, subset).start()

    def small_copy(step):
        return pltpu.make_async_remote_copy(
            src_ref=small_sum.at[step],
            dst_ref=small_got.at[step],
            send_sem=small_send.at[step],
            recv_sem=small_recv.at[step],
            device_id=fellows[step],
            device_id_type=pl.DeviceIdType.MESH,
        )

    def small_step(step):
        if step:
            small_copy(step - 1).wait()
            small_sum[step] = small_sum[step - 1] + small_got[step - 1]
        if step < len(fellows):
            small_copy(step).start()
        else:
            small_out[...] = small_sum[step]

    stages = [fresh, loads, first_sum, lambda j: half_copy(j, 0).start()]
    for step in range(bits):

        def stage(j, step=step):
            half_sum(j, step)
            if step + 1 < bits:
                half_copy(j, step + 1).start()
            else:
                send_along(j)

        stages.append(stage)
    stages.append(last_sum)
    for size in range(1, bits + 1):
        stages.append(lambda j, size=size: pass_on(j, size))
    stages.append(lambda j: local_copy(j).wait())
    order = list(range(3, len(stages))) + [2, 1, 0]

    def round_of(now, carry):
        for step in range(len(fellows) + 1):

            @pl.when(now == step)
            def _(step=step):
                small_step(step)

        for number in order:
            chunk = now - number

            @pl.when((chunk >= 0) & (chunk < count))
            def _(number=number, chunk=chunk):
                stages[number](chunk)

        return carry

    small_sum[0] = small[...]
    lax.fori_loop(0, count + len(stages) - 1, round_of, 0)


def reduced(terms, small, chips, bits, count, number):
    rows, width = terms.shape[0] // (2 * chips), terms.shape[1]
    seq, wide = 1 << bits, width // count
    piece = rows // seq
    slots = bits + 5
    dma = pltpu.SemaphoreType.DMA
    steps = 1 + bits + (chips - 1).bit_length()
    out, _, small_out = pl.pallas_call(
        functools.partial(reduce_kernel, chips, bits, count),
        out_shape=(
            jax.ShapeDtypeStruct((rows, width), BF16),
            jax.ShapeDtypeStruct((count, chips, rows, wide), BF16),
            jax.ShapeDtypeStruct(small.shape, F32),
        ),
        in_specs=[pl.BlockSpec(memory_space=pl.ANY), pl.BlockSpec(memory_space=pltpu.VMEM)],
        out_specs=(
            pl.BlockSpec(memory_space=pl.ANY),
            pl.BlockSpec(memory_space=pl.ANY),
            pl.BlockSpec(memory_space=pltpu.VMEM),
        ),
        scratch_shapes=[pltpu.VMEM((count, chips, rows >> (step + 1), wide), BF16) for step in range(bits)]
        + [
            pltpu.VMEM((slots, chips, rows, wide), BF16),
            pltpu.VMEM((2, chips, rows, wide), BF16),
            pltpu.VMEM((count, chips - 1, piece, wide), BF16),
            pltpu.VMEM((count, piece, wide), BF16),
            dma((count,)),
            dma((count,)),
            dma((count,)),
            dma((count,)),
            dma((count, bits)),
            dma((count, bits)),
            dma((count, chips - 1)),
            dma((count, chips - 1)),
            dma((count, seq - 1)),
            dma((count, seq - 1)),
            dma((count,)),
            pltpu.VMEM((steps + 1,) + small.shape, F32),
            pltpu.VMEM((steps,) + small.shape, F32),
            dma((steps,)),
            dma((steps,)),
        ],
        compiler_params=pltpu.CompilerParams(
            collective_id=number, has_side_effects=True, vmem_limit_bytes=62 * 1024 * 1024
        ),
        cost_estimate=pl.CostEstimate(flops=0, bytes_accessed=800_000_000, transcendentals=0),
    )(terms.reshape(chips, 2, rows, width), small)
    return out, small_out


def gather_kernel(chips, bits, units, weights, ahead, *refs):
    shards, wholes = refs[:weights], refs[weights : 2 * weights]
    held = refs[2 * weights : 3 * weights]
    (in_sem, own_sem, along_out, along_in, spread_out, spread_in, turn_out, turn_in) = refs[3 * weights :]
    here = Place(chips, bits)
    seq = 1 << bits

    barrier = pltpu.get_barrier_semaphore()
    peers = [here.sibling()] + [here.partner(i) for i in range(bits)] + [here.chip(k) for k in range(1, chips)]
    for peer in peers:
        pl.semaphore_signal(barrier, inc=1, device_id=peer, device_id_type=pl.DeviceIdType.MESH)
    pl.semaphore_wait(barrier, len(peers))

    def rows_of(unit, shift):
        which, first, width = units[unit]
        count = shards[which].shape[0]
        row = (((here.z - shift) % chips) * 2 + here.core) * count
        return which, row, count, first, width

    def piece_of(unit, shift, subset):
        which, row, count, first, width = rows_of(unit, shift)
        part = here.part_of(subset)
        if (count // seq) % 16 == 0:
            size = count // seq
            return which, pl.ds(pl.multiple_of(row + part * size, 16), size), pl.ds(first, width)
        size = width // seq
        return which, pl.ds(pl.multiple_of(row, 16), count), pl.ds(pl.multiple_of(first + part * size, 128), size)

    def remote(source, target, sems, index, device):
        return pltpu.make_async_remote_copy(
            src_ref=source,
            dst_ref=target,
            send_sem=sems[0].at[index],
            recv_sem=sems[1].at[index],
            device_id=device,
            device_id_type=pl.DeviceIdType.MESH,
        )

    def along(unit, k):
        which, row, count, first, width = rows_of(unit, 0)
        _, there, columns = piece_of(unit, 0, 0)
        part = here.part
        if (count // seq) % 16 == 0:
            size = count // seq
            source = shards[which].at[pl.ds(pl.multiple_of(part * size, 16), size), columns]
        else:
            source = shards[which].at[:, columns]
        return remote(source, wholes[which].at[there, columns], (along_out, along_in), (unit, k - 1), here.chip(k))

    def spread(unit, k, subset):
        last = subset.bit_length() - 1
        which, there, columns = piece_of(unit, k, subset ^ (1 << last))
        region = wholes[which].at[there, columns]
        return remote(region, region, (spread_out, spread_in), (unit, k - 1, subset - 1), here.partner(last))

    def turn(unit, k):
        which, row, count, first, width = rows_of(unit, k)
        there = pl.ds(pl.multiple_of(row, 16), count)
        region = wholes[which].at[there, pl.ds(first, width)]
        source = region if k else shards[which].at[:, pl.ds(first, width)]
        return remote(source, region, (turn_out, turn_in), (unit, k), here.sibling())

    def load(which):
        return pltpu.make_async_copy(shards[which], held[which], in_sem.at[which])

    def store(which):
        count = shards[which].shape[0]
        row = (here.z * 2 + here.core) * count
        there = pl.ds(pl.multiple_of(row, 16), count)
        return pltpu.make_async_copy(held[which], wholes[which].at[there], own_sem.at[which])

    def level(size):
        return [subset for subset in range(1, seq) if bin(subset).count("1") == size]

    shifts = range(1, chips)

    def begin(unit):
        for k in shifts:
            along(unit, k).start()
        turn(unit, 0).start()

    def arrive(unit):
        for k in shifts:
            along(unit, k).wait()
            for subset in level(1):
                spread(unit, k, subset).start()

    def pass_on(unit, size):
        for k in shifts:
            for subset in level(size):
                spread(unit, k, subset).wait()
            for subset in level(size + 1):
                spread(unit, k, subset).start()
            if size == bits:
                turn(unit, k).start()

    def finish(unit):
        for k in range(chips):
            turn(unit, k).wait()

    for which in range(weights):
        load(which).start()
    stages = [arrive]
    for size in range(1, bits + 1):
        stages.append(lambda unit, size=size: pass_on(unit, size))
    stages.append(finish)
    for unit in range(min(ahead, len(units))):
        begin(unit)
    for now in range(len(units) + len(stages) - 1):
        if now + ahead < len(units):
            begin(now + ahead)
        for number, stage in enumerate(stages):
            unit = now - number
            if 0 <= unit < len(units):
                stage(unit)
        if now < weights:
            load(now).wait()
            store(now).start()
    for which in range(weights):
        if which >= len(units) + len(stages) - 1:
            load(which).wait()
            store(which).start()
    for which in range(weights):
        store(which).wait()


def gathered(shards, chips, bits, units, ahead):
    weights, seq, count = len(shards), 1 << bits, len(units)
    dma = pltpu.SemaphoreType.DMA
    return pl.pallas_call(
        functools.partial(gather_kernel, chips, bits, units, weights, ahead),
        out_shape=tuple(jax.ShapeDtypeStruct((2 * chips * one.shape[0], one.shape[1]), one.dtype) for one in shards),
        in_specs=[pl.BlockSpec(memory_space=pl.ANY)] * weights,
        out_specs=tuple(pl.BlockSpec(memory_space=pl.ANY) for _ in shards),
        scratch_shapes=[pltpu.VMEM(one.shape, one.dtype) for one in shards]
        + [
            dma((weights,)),
            dma((weights,)),
            dma((count, chips - 1)),
            dma((count, chips - 1)),
            dma((count, chips - 1, seq - 1)),
            dma((count, chips - 1, seq - 1)),
            dma((count, chips)),
            dma((count, chips)),
        ],
        compiler_params=pltpu.CompilerParams(
            collective_id=1, has_side_effects=True, vmem_limit_bytes=62 * 1024 * 1024
        ),
        cost_estimate=pl.CostEstimate(flops=0, bytes_accessed=900_000_000, transcendentals=0),
    )(*shards)


def parts_of(which, width, count):
    return tuple((which, i * (width // count), width // count) for i in range(count))


class Plane:
    def __init__(self):
        self.seq = lax.axis_size("seq")
        self.batch = lax.axis_size("batch")
        self.chips = self.batch // 2
        self.bits = self.seq.bit_length() - 1
        self.core = lax.axis_index("batch") % 2
        s = lax.axis_index("seq")
        self.reversed = [self.reverse(i) for i in range(self.seq)]
        self.part = jnp.where(self.core == 0, self.reverse(s), s)

    def reverse(self, value):
        return sum(((value >> bit) & 1) << (self.bits - 1 - bit) for bit in range(self.bits))

    def send(self, array, target):
        pairs = []
        for s in range(self.seq):
            for z in range(self.chips):
                for core in range(2):
                    there, to = target(core, s)
                    pairs.append((s * self.batch + z * 2 + core, to * self.batch + z * 2 + there))
        return lax.ppermute(array, ("seq", "batch"), pairs)

    def swap_cores(self, array):
        return self.send(array, lambda core, s: (1 - core, s))

    def stage(self, array, step):
        masks = (1 << step, 1 << (self.bits - 1 - step))
        return self.send(array, lambda core, s: (core, s ^ masks[core]))


class Fold:
    def __init__(self, terms):
        self.plane = Plane()
        chips = self.plane.chips
        self.rows, self.width = terms.shape[0] // (2 * chips), terms.shape[1]
        self.terms = terms.reshape(chips, 2, self.rows, self.width)
        self.first, self.size, self.step = 0, self.rows, 0
        self.held = []
        away = self.mine(1 - self.plane.core, 0, self.rows)
        self.pending = self.plane.swap_cores(away)

    def mine(self, core, first, size):
        shape = (self.plane.chips, 1, size, self.width)
        return lax.dynamic_slice(self.terms, (0, core, first, 0), shape)[:, 0]

    def total(self, first, size):
        shape = (self.plane.chips, size, self.width)
        total = self.mine(self.plane.core, first, size).astype(F32)
        for array, base in self.held:
            total = total + lax.dynamic_slice(array, (0, first - base, 0), shape).astype(F32)
        return total.astype(BF16)

    def advance(self, *values):
        pending, *values = lax.optimization_barrier((self.pending, *values))
        self.held.append((pending, self.first))
        half = self.size // 2
        bit = (self.plane.part >> (self.plane.bits - 1 - self.step)) & 1
        leave, *values = lax.optimization_barrier((self.total(self.first + (1 - bit) * half, half), *values))
        self.first, self.size = self.first + bit * half, half
        self.pending = self.plane.stage(leave, self.step)
        self.step += 1
        return values

    def finish(self, *values):
        while self.step < self.plane.bits:
            values = self.advance(*values)
        pending, *values = lax.optimization_barrier((self.pending, *values))
        self.held.append((pending, self.first))
        return self.total(self.first, self.size), *values

    def spread(self, mine):
        parts = lax.all_gather(mine, "seq")
        turned = jnp.stack([parts[i] for i in self.plane.reversed])
        return jnp.where(self.plane.core == 0, turned, parts).reshape(self.rows, self.width)


def scatter_rows(terms):
    return lax.psum_scatter(terms, "batch", scatter_dimension=0, tiled=True)


def local(
    tokens,
    cotangent,
    segment_ids,
    positions,
    attn_gain,
    qkv_weight,
    out_weight,
    mlp_gain,
    gate_up_weight,
    down_weight,
):
    seq = lax.axis_size("seq")
    chips = lax.axis_size("batch") // 2
    bits = seq.bit_length() - 1
    s = lax.axis_index("seq")
    swap = [(i, i ^ 1) for i in range(seq)]
    model_width = tokens.shape[2]
    rows = tokens.shape[1]
    if rows * 2 != DOC_MAX:
        raise ValueError("token shard")
    share = H // KV
    kv_width = KV * HD
    scale_factor = HD ** (-0.5)
    ff_width = gate_up_weight.shape[1] // 2

    shards = (qkv_weight, out_weight, gate_up_weight, down_weight)
    cuts = (2, 2, 8, max(1, min(4, model_width // (seq * 128))))
    units = sum((parts_of(i, one.shape[1], n) for i, (one, n) in enumerate(zip(shards, cuts))), ())
    qkv_whole, out_whole, gate_up_whole, down_whole = gathered(shards, chips, bits, units, 3)

    inputs = tokens[0].astype(F32)
    normed, inv_first = rms_parts(inputs, attn_gain)
    normed_low = normed.astype(BF16)
    projected = dot(normed_low, qkv_whole)

    row_start = s * rows
    own_segments = lax.dynamic_slice_in_dim(segment_ids[0], row_start, rows, 0)
    other = s ^ 1
    other_segments = lax.dynamic_slice_in_dim(segment_ids[0], other * rows, rows, 0)
    own_positions = lax.dynamic_slice_in_dim(positions[0], row_start, rows, 0)
    cosine, sine_part = rotary_tables(own_positions, HD)
    queries = projected[:, :model_width].astype(BF16).reshape(rows, H, HD)
    queries_rot = rotate(queries.astype(F32), cosine, sine_part).astype(BF16)
    queries_rot = queries_rot.reshape(rows, KV, share, HD)
    keys = projected[:, model_width : model_width + kv_width].astype(BF16).reshape(rows, KV, HD)
    keys_rot = rotate(keys.astype(F32), cosine, sine_part).astype(BF16).reshape(rows, kv_width)
    values = projected[:, model_width + kv_width :].astype(BF16)
    own_kv = jnp.concatenate([keys_rot, values], axis=1)
    other_kv = lax.ppermute(own_kv, "seq", swap)
    both_kv = jnp.concatenate([own_kv, other_kv], axis=0)
    all_keys = both_kv[:, :kv_width].reshape(2 * rows, KV, HD)
    all_values = both_kv[:, kv_width:].reshape(2 * rows, KV, HD)
    index = jnp.arange(rows, dtype=jnp.int32)
    allowed = jnp.concatenate(
        [
            (index[None, :] <= index[:, None]) & (own_segments[None, :] == own_segments[:, None]),
            (other < s) & (other_segments[None, :] == own_segments[:, None]),
        ],
        axis=1,
    )
    scores = (
        jnp.einsum("qgsd,kgd->gsqk", queries_rot, all_keys, preferred_element_type=F32)
        * scale_factor
    )
    masked = jnp.where(allowed[None, None], scores, -1e30)
    row_max = jnp.max(masked, axis=-1, keepdims=True)
    exps = jnp.exp(masked - row_max)
    probs = exps / jnp.sum(exps, axis=-1, keepdims=True)
    probs_low = probs.astype(BF16)
    attended = jnp.einsum("gsqk,kgd->qgsd", probs_low, all_values, preferred_element_type=F32)
    attended = attended.astype(BF16).reshape(rows, model_width)
    residual = inputs + dot(attended, out_whole)
    normed_mlp, inv_second = rms_parts(residual, mlp_gain)
    normed_mlp_low = normed_mlp.astype(BF16)
    gate_up = dot(normed_mlp_low, gate_up_whole)
    gate_part = gate_up[:, :ff_width]
    up_part = gate_up[:, ff_width:]
    sigmoid_gate = jax.nn.sigmoid(gate_part)
    hidden_low = (gate_part * sigmoid_gate * up_part).astype(BF16)
    output = (residual + dot(hidden_low, down_whole)).astype(BF16)

    grad_out = cotangent[0].astype(F32)
    grad_down = cotangent[0]
    down_terms, grad_down = lax.optimization_barrier((dot_tn(hidden_low, grad_down).astype(BF16), grad_down))
    down_fold = Fold(down_terms)
    grad_hidden = dot_nt(grad_down, down_whole)
    grad_gate = grad_hidden * up_part * sigmoid_gate * (1.0 + gate_part * (1.0 - sigmoid_gate))
    grad_up = grad_hidden * gate_part * sigmoid_gate
    grad_gate_up = jnp.concatenate([grad_gate, grad_up], axis=1).astype(BF16)
    grad_normed_mlp = dot_nt(grad_gate_up, gate_up_whole)
    mlp_term = jnp.sum(grad_normed_mlp * residual * inv_second, axis=0)
    grad_resid = grad_out + norm_back(grad_normed_mlp, residual, inv_second, mlp_gain)
    (grad_proj,) = down_fold.advance(grad_resid.astype(BF16))
    out_part = scatter_rows(dot_tn(attended, grad_proj).astype(BF16))
    grad_heads = dot_nt(grad_proj, out_whole)
    grad_heads = grad_heads.astype(BF16).reshape(rows, KV, share, HD)

    grad_probs = jnp.einsum("qgsd,kgd->gsqk", grad_heads, all_values, preferred_element_type=F32)
    inner_sum = jnp.sum(probs * grad_probs, axis=-1, keepdims=True)
    grad_scores = (probs * (grad_probs - inner_sum)).astype(BF16)
    grad_queries = (
        jnp.einsum("gsqk,kgd->qgsd", grad_scores, all_keys, preferred_element_type=F32)
        * scale_factor
    )
    grad_keys = (
        jnp.einsum("gsqk,qgsd->kgd", grad_scores, queries_rot, preferred_element_type=F32)
        * scale_factor
    )
    grad_values = jnp.einsum("gsqk,qgsd->kgd", probs_low, grad_heads, preferred_element_type=F32)
    grad_kv = jnp.concatenate(
        [grad_keys.reshape(2 * rows, kv_width), grad_values.reshape(2 * rows, kv_width)], axis=1
    )
    away = grad_kv[rows:].astype(BF16)
    arrived = lax.ppermute(away, "seq", swap)
    own_grad_kv = grad_kv[:rows] + arrived.astype(F32)
    back_queries = rotate(grad_queries.reshape(rows, H, HD), cosine, -sine_part)
    back_keys = rotate(own_grad_kv[:, :kv_width].reshape(rows, KV, HD), cosine, -sine_part)
    grad_qkv = jnp.concatenate(
        [
            back_queries.reshape(rows, model_width),
            back_keys.reshape(rows, kv_width),
            own_grad_kv[:, kv_width:],
        ],
        axis=1,
    ).astype(BF16)
    if down_fold.step < bits:
        (grad_qkv,) = down_fold.advance(grad_qkv)
    qkv_part = scatter_rows(dot_tn(normed_low, grad_qkv).astype(BF16))
    grad_normed = dot_nt(grad_qkv, qkv_whole)
    attn_term = jnp.sum(grad_normed * inputs * inv_first, axis=0)
    tokens_grad = (grad_resid + norm_back(grad_normed, inputs, inv_first, attn_gain)).astype(BF16)
    gains = jnp.concatenate([attn_term, mlp_term]).reshape(-1, 128)
    normed_mlp_low, gains = lax.optimization_barrier((normed_mlp_low, gains))
    gate_up_terms = dot_tn(normed_mlp_low, grad_gate_up).astype(BF16)
    out_grad = lax.psum(out_part, "seq")
    down_part, gate_up_terms = down_fold.finish(gate_up_terms)
    groups = [list(range(core, 2 * chips, 2)) for core in range(2)]
    down_part = lax.psum_scatter(down_part, "batch", scatter_dimension=0, axis_index_groups=groups)
    gate_up_grad, gains = reduced(gate_up_terms, gains, chips, bits, 11, 0)
    gains = gains.reshape(-1)
    gate_up_grad, out_grad, qkv_part, down_part = lax.optimization_barrier(
        (gate_up_grad, out_grad, qkv_part, down_part)
    )
    qkv_grad = lax.psum(qkv_part, "seq")
    down_grad = down_fold.spread(down_part)
    return (
        output[None],
        tokens_grad[None],
        gains[:model_width],
        qkv_grad.astype(F32),
        out_grad.astype(F32),
        gains[model_width:],
        gate_up_grad.astype(F32),
        down_grad.astype(F32),
    )


def solution(mesh):
    return jax.shard_map(
        local,
        mesh=mesh,
        in_specs=(
            P("batch", "seq", None),
            P("batch", "seq", None),
            P("batch", None),
            P("batch", None),
            P(),
            P("batch", None),
            P("batch", None),
            P(),
            P("batch", None),
            P("batch", None),
        ),
        out_specs=(
            P("batch", "seq", None),
            P("batch", "seq", None),
            P(),
            P("batch", None),
            P("batch", None),
            P(),
            P("batch", None),
            P("batch", None),
        ),
        check_vma=False,
    )
```

```python
import functools

import jax
import jax.numpy as jnp
from jax import lax
from jax.experimental import pallas as pl
from jax.experimental.pallas import tpu as pltpu
from jax.sharding import PartitionSpec as P

H = 32
KV = 4
HD = 64
DOC_MAX = 512
F32 = jnp.float32
BF16 = jnp.bfloat16


def rms_parts(values, gain_vector):
    inv_rms = lax.rsqrt(jnp.mean(values * values, axis=-1, keepdims=True) + 1e-05)
    return (values * inv_rms * gain_vector, inv_rms)


def norm_back(grad_normed, values, inv_rms, gain_vector):
    weighted = grad_normed * gain_vector
    inner_sum = jnp.mean(weighted * values, axis=-1, keepdims=True)
    return inv_rms * weighted - values * (inv_rms * inv_rms * inv_rms) * inner_sum


def rotary_tables(seq_positions, head_dim):
    half_dim = head_dim // 2
    frequency = 10000.0 ** (-jnp.arange(half_dim, dtype=F32) * 2.0 / head_dim)
    angles = seq_positions.astype(F32)[:, None] * frequency[None, :]
    return (jnp.cos(angles)[:, None, :], jnp.sin(angles)[:, None, :])


def rotate(values, cosine, sine_part):
    half_dim = values.shape[-1] // 2
    first_half = values[..., :half_dim]
    second_half = values[..., half_dim:]
    return jnp.concatenate(
        [
            first_half * cosine - second_half * sine_part,
            second_half * cosine + first_half * sine_part,
        ],
        axis=-1,
    )


def dot(left, right):
    return jnp.dot(left, right, preferred_element_type=F32)


def dot_nt(left, right):
    return lax.dot_general(left, right, (((1,), (1,)), ((), ())), preferred_element_type=F32)


def dot_tn(left, right):
    return lax.dot_general(left, right, (((0,), (0,)), ((), ())), preferred_element_type=F32)


class Place:
    def __init__(self, chips, bits):
        self.chips, self.bits = chips, bits
        self.s = lax.axis_index("seq")
        place = lax.axis_index("batch")
        self.z, self.core = place // 2, place % 2
        reverse = 0
        for bit in range(bits):
            reverse = reverse + ((self.s // (1 << bit)) % 2) * (1 << (bits - 1 - bit))
        self.part = reverse + self.core * (self.s - reverse)

    def sibling(self):
        return {"batch": self.z * 2 + 1 - self.core}

    def chip(self, shift):
        return {"batch": ((self.z + shift) % self.chips) * 2 + self.core}

    def partner(self, step):
        first, second = 1 << step, 1 << (self.bits - 1 - step)
        mask = first + self.core * (second - first)
        return {"seq": self.s + mask * (1 - 2 * ((self.s // mask) % 2))}

    def fellows(self):
        found = [self.sibling()] + [self.partner(step) for step in range(self.bits)]
        step = 1
        while step < self.chips:
            found.append({"batch": (self.z + step * (1 - 2 * ((self.z // step) % 2))) * 2 + self.core})
            step *= 2
        return found

    def bit(self, step):
        return (self.part // (1 << (self.bits - 1 - step))) % 2

    def part_of(self, subset):
        part = self.part
        for step in range(self.bits):
            if subset >> step & 1:
                weight = 1 << (self.bits - 1 - step)
                part = part + weight * (1 - 2 * self.bit(step))
        return part


def reduce_kernel(chips, bits, counts, *refs):
    terms, small, outs, arrived, small_out, scratch = refs[:2], refs[2], refs[3:5], refs[5], refs[6], refs[7:]
    count = sum(counts)
    halves = scratch[:bits]
    own, got, along, final = scratch[bits : bits + 4]
    (own_sem, got_sem, core_out, core_in, half_out, half_in, along_out, along_in, spread_out, spread_in, local_sem) = (
        scratch[bits + 4 : -4]
    )
    small_sum, small_got, small_send, small_recv = scratch[-4:]
    here = Place(chips, bits)
    rows, width = own.shape[2], own.shape[3]
    piece = rows >> bits
    slots = own.shape[0]
    seq = 1 << bits

    barrier = pltpu.get_barrier_semaphore()
    peers = [here.sibling()] + [here.partner(i) for i in range(bits)] + [here.chip(k) for k in range(1, chips)]
    fellows = here.fellows()
    for peer in peers:
        pl.semaphore_signal(barrier, inc=1, device_id=peer, device_id_type=pl.DeviceIdType.MESH)
    pl.semaphore_wait(barrier, len(peers))

    def columns(column):
        return pl.ds(pl.multiple_of(column * width, 128), width)

    def launch(make, j):
        @pl.when(j < counts[0])
        def _():
            make(j, 0, j).start()

        @pl.when(j >= counts[0])
        def _():
            make(j, 1, j - counts[0]).start()

    def core_copy(j, which=0, column=0):
        return pltpu.make_async_remote_copy(
            src_ref=terms[which].at[:, 1 - here.core, :, columns(column)],
            dst_ref=arrived.at[j],
            send_sem=core_out.at[j],
            recv_sem=core_in.at[j],
            device_id=here.sibling(),
            device_id_type=pl.DeviceIdType.MESH,
        )

    def own_load(j, which=0, column=0):
        return pltpu.make_async_copy(
            terms[which].at[:, here.core, :, columns(column)], own.at[j % slots], own_sem.at[j]
        )

    def got_load(j):
        return pltpu.make_async_copy(arrived.at[j], got.at[j % 2], got_sem.at[j])

    def offset(step):
        total = 0
        for i in range(step):
            total = total + here.bit(i) * (rows >> (i + 1))
        return total

    def half_copy(j, step):
        half = rows >> (step + 1)
        first = pl.multiple_of(offset(step) + (1 - here.bit(step)) * half, piece)
        return pltpu.make_async_remote_copy(
            src_ref=own.at[j % slots, :, pl.ds(first, half), :],
            dst_ref=halves[step].at[j],
            send_sem=half_out.at[j, step],
            recv_sem=half_in.at[j, step],
            device_id=here.partner(step),
            device_id_type=pl.DeviceIdType.MESH,
        )

    def along_copy(j, k):
        first = pl.multiple_of(offset(bits), piece)
        return pltpu.make_async_remote_copy(
            src_ref=own.at[j % slots, (here.z + k) % chips, pl.ds(first, piece), :],
            dst_ref=along.at[j, k - 1],
            send_sem=along_out.at[j, k - 1],
            recv_sem=along_in.at[j, k - 1],
            device_id=here.chip(k),
            device_id_type=pl.DeviceIdType.MESH,
        )

    def place_of(which, column, subset):
        first = pl.multiple_of(here.part_of(subset) * piece, piece)
        return outs[which].at[pl.ds(first, piece), columns(column)]

    def spread_copy(subset, j, which=0, column=0):
        last = subset.bit_length() - 1
        parent = subset ^ (1 << last)
        return pltpu.make_async_remote_copy(
            src_ref=final.at[j] if parent == 0 else place_of(which, column, parent),
            dst_ref=place_of(which, column, parent),
            send_sem=spread_out.at[j, subset - 1],
            recv_sem=spread_in.at[j, subset - 1],
            device_id=here.partner(last),
            device_id_type=pl.DeviceIdType.MESH,
        )

    def local_copy(j, which=0, column=0):
        return pltpu.make_async_copy(final.at[j], place_of(which, column, 0), local_sem.at[j])

    def level(size):
        return [subset for subset in range(1, seq) if bin(subset).count("1") == size]

    def fresh(j):
        launch(core_copy, j)

    def loads(j):
        core_copy(j).wait()
        launch(own_load, j)
        got_load(j).start()

    def first_sum(j):
        own_load(j).wait()
        got_load(j).wait()
        block = 32 if rows % 32 == 0 else 16
        blocks = rows // block
        slot = j % slots

        def body(index, carry):
            z = index // blocks
            span = pl.ds(pl.multiple_of((index % blocks) * block, block), block)
            own[slot, z, span, :] = (
                own[slot, z, span, :].astype(F32) + got[j % 2, z, span, :].astype(F32)
            ).astype(BF16)
            return carry

        lax.fori_loop(0, chips * blocks, body, 0)

    def half_sum(j, step):
        half_copy(j, step).wait()
        half = rows >> (step + 1)
        block = 32 if half % 32 == 0 else 16
        blocks = half // block
        slot = j % slots
        start = offset(step + 1)

        def body(index, carry):
            z = index // blocks
            first = (index % blocks) * block
            there = pl.ds(pl.multiple_of(first, block), block)
            span = pl.ds(pl.multiple_of(start + first, block), block)
            own[slot, z, span, :] = (
                own[slot, z, span, :].astype(F32) + halves[step][j, z, there, :].astype(F32)
            ).astype(BF16)
            return carry

        lax.fori_loop(0, chips * blocks, body, 0)

    def send_along(j):
        for k in range(1, chips):
            along_copy(j, k).start()

    def last_sum(j):
        for k in range(1, chips):
            along_copy(j, k).wait()
        block = 16
        slot = j % slots
        start = offset(bits)

        def body(index, carry):
            first = index * block
            there = pl.ds(pl.multiple_of(first, block), block)
            total = own[slot, here.z, pl.ds(pl.multiple_of(start + first, block), block), :].astype(F32)
            for k in range(chips - 1):
                total = total + along[j, k, there, :].astype(F32)
            final[j, there, :] = total.astype(BF16)
            return carry

        lax.fori_loop(0, piece // block, body, 0)
        launch(local_copy, j)
        for subset in level(1):
            launch(functools.partial(spread_copy, subset), j)

    def pass_on(j, size):
        for subset in level(size):
            spread_copy(subset, j).wait()
        for subset in level(size + 1):
            launch(functools.partial(spread_copy, subset), j)

    def small_copy(step):
        return pltpu.make_async_remote_copy(
            src_ref=small_sum.at[step],
            dst_ref=small_got.at[step],
            send_sem=small_send.at[step],
            recv_sem=small_recv.at[step],
            device_id=fellows[step],
            device_id_type=pl.DeviceIdType.MESH,
        )

    def small_step(step):
        if step:
            small_copy(step - 1).wait()
            small_sum[step] = small_sum[step - 1] + small_got[step - 1]
        if step < len(fellows):
            small_copy(step).start()
        else:
            small_out[...] = small_sum[step]

    stages = [fresh, loads, first_sum, lambda j: half_copy(j, 0).start()]
    for step in range(bits):

        def stage(j, step=step):
            half_sum(j, step)
            if step + 1 < bits:
                half_copy(j, step + 1).start()
            else:
                send_along(j)

        stages.append(stage)
    stages.append(last_sum)
    for size in range(1, bits + 1):
        stages.append(lambda j, size=size: pass_on(j, size))
    stages.append(lambda j: local_copy(j).wait())
    order = list(range(3, len(stages))) + [2, 1, 0]

    def round_of(now, carry):
        for step in range(len(fellows) + 1):

            @pl.when(now == step)
            def _(step=step):
                small_step(step)

        for number in order:
            chunk = now - number

            @pl.when((chunk >= 0) & (chunk < count))
            def _(number=number, chunk=chunk):
                stages[number](chunk)

        return carry

    small_sum[0] = small[...]
    lax.fori_loop(0, count + len(stages) - 1, round_of, 0)


def reduced(terms, small, chips, bits, wide):
    rows = terms[0].shape[0] // (2 * chips)
    widths = [one.shape[1] for one in terms]
    counts = [width // wide for width in widths]
    count, seq = sum(counts), 1 << bits
    piece = rows // seq
    slots = bits + 5
    dma = pltpu.SemaphoreType.DMA
    steps = 1 + bits + (chips - 1).bit_length()
    *outs, _, small_out = pl.pallas_call(
        functools.partial(reduce_kernel, chips, bits, counts),
        out_shape=(
            *[jax.ShapeDtypeStruct((rows, width), BF16) for width in widths],
            jax.ShapeDtypeStruct((count, chips, rows, wide), BF16),
            jax.ShapeDtypeStruct(small.shape, F32),
        ),
        in_specs=[pl.BlockSpec(memory_space=pl.ANY)] * 2 + [pl.BlockSpec(memory_space=pltpu.VMEM)],
        out_specs=(
            pl.BlockSpec(memory_space=pl.ANY),
            pl.BlockSpec(memory_space=pl.ANY),
            pl.BlockSpec(memory_space=pl.ANY),
            pl.BlockSpec(memory_space=pltpu.VMEM),
        ),
        scratch_shapes=[pltpu.VMEM((count, chips, rows >> (step + 1), wide), BF16) for step in range(bits)]
        + [
            pltpu.VMEM((slots, chips, rows, wide), BF16),
            pltpu.VMEM((2, chips, rows, wide), BF16),
            pltpu.VMEM((count, chips - 1, piece, wide), BF16),
            pltpu.VMEM((count, piece, wide), BF16),
            dma((count,)),
            dma((count,)),
            dma((count,)),
            dma((count,)),
            dma((count, bits)),
            dma((count, bits)),
            dma((count, chips - 1)),
            dma((count, chips - 1)),
            dma((count, seq - 1)),
            dma((count, seq - 1)),
            dma((count,)),
            pltpu.VMEM((steps + 1,) + small.shape, F32),
            pltpu.VMEM((steps,) + small.shape, F32),
            dma((steps,)),
            dma((steps,)),
        ],
        compiler_params=pltpu.CompilerParams(
            collective_id=0, has_side_effects=True, vmem_limit_bytes=62 * 1024 * 1024
        ),
        cost_estimate=pl.CostEstimate(flops=0, bytes_accessed=800_000_000, transcendentals=0),
    )(*[one.reshape(chips, 2, rows, -1) for one in terms], small)
    return *outs, small_out


def gather_kernel(chips, bits, units, weights, ahead, *refs):
    shards, wholes = refs[:weights], refs[weights : 2 * weights]
    held = refs[2 * weights : 3 * weights]
    (in_sem, own_sem, along_out, along_in, spread_out, spread_in, turn_out, turn_in) = refs[3 * weights :]
    here = Place(chips, bits)
    seq = 1 << bits

    barrier = pltpu.get_barrier_semaphore()
    peers = [here.sibling()] + [here.partner(i) for i in range(bits)] + [here.chip(k) for k in range(1, chips)]
    for peer in peers:
        pl.semaphore_signal(barrier, inc=1, device_id=peer, device_id_type=pl.DeviceIdType.MESH)
    pl.semaphore_wait(barrier, len(peers))

    def rows_of(unit, shift):
        which, first, width = units[unit]
        count = shards[which].shape[0]
        row = (((here.z - shift) % chips) * 2 + here.core) * count
        return which, row, count, first, width

    def piece_of(unit, shift, subset):
        which, row, count, first, width = rows_of(unit, shift)
        part = here.part_of(subset)
        if (count // seq) % 16 == 0:
            size = count // seq
            return which, pl.ds(pl.multiple_of(row + part * size, 16), size), pl.ds(first, width)
        size = width // seq
        return which, pl.ds(pl.multiple_of(row, 16), count), pl.ds(pl.multiple_of(first + part * size, 128), size)

    def remote(source, target, sems, index, device):
        return pltpu.make_async_remote_copy(
            src_ref=source,
            dst_ref=target,
            send_sem=sems[0].at[index],
            recv_sem=sems[1].at[index],
            device_id=device,
            device_id_type=pl.DeviceIdType.MESH,
        )

    def along(unit, k):
        which, row, count, first, width = rows_of(unit, 0)
        _, there, columns = piece_of(unit, 0, 0)
        part = here.part
        if (count // seq) % 16 == 0:
            size = count // seq
            source = shards[which].at[pl.ds(pl.multiple_of(part * size, 16), size), columns]
        else:
            source = shards[which].at[:, columns]
        return remote(source, wholes[which].at[there, columns], (along_out, along_in), (unit, k - 1), here.chip(k))

    def spread(unit, k, subset):
        last = subset.bit_length() - 1
        which, there, columns = piece_of(unit, k, subset ^ (1 << last))
        region = wholes[which].at[there, columns]
        return remote(region, region, (spread_out, spread_in), (unit, k - 1, subset - 1), here.partner(last))

    def turn(unit, k):
        which, row, count, first, width = rows_of(unit, k)
        there = pl.ds(pl.multiple_of(row, 16), count)
        region = wholes[which].at[there, pl.ds(first, width)]
        source = region if k else shards[which].at[:, pl.ds(first, width)]
        return remote(source, region, (turn_out, turn_in), (unit, k), here.sibling())

    def load(which):
        return pltpu.make_async_copy(shards[which], held[which], in_sem.at[which])

    def store(which):
        count = shards[which].shape[0]
        row = (here.z * 2 + here.core) * count
        there = pl.ds(pl.multiple_of(row, 16), count)
        return pltpu.make_async_copy(held[which], wholes[which].at[there], own_sem.at[which])

    def level(size):
        return [subset for subset in range(1, seq) if bin(subset).count("1") == size]

    shifts = range(1, chips)

    def begin(unit):
        for k in shifts:
            along(unit, k).start()
        turn(unit, 0).start()

    def arrive(unit):
        for k in shifts:
            along(unit, k).wait()
            for subset in level(1):
                spread(unit, k, subset).start()

    def pass_on(unit, size):
        for k in shifts:
            for subset in level(size):
                spread(unit, k, subset).wait()
            for subset in level(size + 1):
                spread(unit, k, subset).start()
            if size == bits:
                turn(unit, k).start()

    def finish(unit):
        for k in range(chips):
            turn(unit, k).wait()

    for which in range(weights):
        load(which).start()
    stages = [arrive]
    for size in range(1, bits + 1):
        stages.append(lambda unit, size=size: pass_on(unit, size))
    stages.append(finish)
    for unit in range(min(ahead, len(units))):
        begin(unit)
    for now in range(len(units) + len(stages) - 1):
        if now + ahead < len(units):
            begin(now + ahead)
        for number, stage in enumerate(stages):
            unit = now - number
            if 0 <= unit < len(units):
                stage(unit)
        if now < weights:
            load(now).wait()
            store(now).start()
    for which in range(weights):
        if which >= len(units) + len(stages) - 1:
            load(which).wait()
            store(which).start()
    for which in range(weights):
        store(which).wait()


def gathered(shards, chips, bits, units, ahead):
    weights, seq, count = len(shards), 1 << bits, len(units)
    dma = pltpu.SemaphoreType.DMA
    return pl.pallas_call(
        functools.partial(gather_kernel, chips, bits, units, weights, ahead),
        out_shape=tuple(jax.ShapeDtypeStruct((2 * chips * one.shape[0], one.shape[1]), one.dtype) for one in shards),
        in_specs=[pl.BlockSpec(memory_space=pl.ANY)] * weights,
        out_specs=tuple(pl.BlockSpec(memory_space=pl.ANY) for _ in shards),
        scratch_shapes=[pltpu.VMEM(one.shape, one.dtype) for one in shards]
        + [
            dma((weights,)),
            dma((weights,)),
            dma((count, chips - 1)),
            dma((count, chips - 1)),
            dma((count, chips - 1, seq - 1)),
            dma((count, chips - 1, seq - 1)),
            dma((count, chips)),
            dma((count, chips)),
        ],
        compiler_params=pltpu.CompilerParams(
            collective_id=1, has_side_effects=True, vmem_limit_bytes=62 * 1024 * 1024
        ),
        cost_estimate=pl.CostEstimate(flops=0, bytes_accessed=900_000_000, transcendentals=0),
    )(*shards)


def parts_of(which, width, count):
    return tuple((which, i * (width // count), width // count) for i in range(count))


class Plane:
    def __init__(self):
        self.seq = lax.axis_size("seq")
        self.batch = lax.axis_size("batch")
        self.chips = self.batch // 2
        self.bits = self.seq.bit_length() - 1
        self.core = lax.axis_index("batch") % 2
        s = lax.axis_index("seq")
        self.reversed = [self.reverse(i) for i in range(self.seq)]
        self.part = jnp.where(self.core == 0, self.reverse(s), s)

    def reverse(self, value):
        return sum(((value >> bit) & 1) << (self.bits - 1 - bit) for bit in range(self.bits))

    def send(self, array, target):
        pairs = []
        for s in range(self.seq):
            for z in range(self.chips):
                for core in range(2):
                    there, to = target(core, s)
                    pairs.append((s * self.batch + z * 2 + core, to * self.batch + z * 2 + there))
        return lax.ppermute(array, ("seq", "batch"), pairs)

    def swap_cores(self, array):
        return self.send(array, lambda core, s: (1 - core, s))

    def stage(self, array, step):
        masks = (1 << step, 1 << (self.bits - 1 - step))
        return self.send(array, lambda core, s: (core, s ^ masks[core]))


class Fold:
    def __init__(self, terms):
        self.plane = Plane()
        chips = self.plane.chips
        self.rows, self.width = terms.shape[0] // (2 * chips), terms.shape[1]
        self.terms = terms.reshape(chips, 2, self.rows, self.width)
        self.first, self.size, self.step = 0, self.rows, 0
        self.held = []
        away = self.mine(1 - self.plane.core, 0, self.rows)
        self.pending = self.plane.swap_cores(away)

    def mine(self, core, first, size):
        shape = (self.plane.chips, 1, size, self.width)
        return lax.dynamic_slice(self.terms, (0, core, first, 0), shape)[:, 0]

    def total(self, first, size):
        shape = (self.plane.chips, size, self.width)
        total = self.mine(self.plane.core, first, size).astype(F32)
        for array, base in self.held:
            total = total + lax.dynamic_slice(array, (0, first - base, 0), shape).astype(F32)
        return total.astype(BF16)

    def advance(self, *values):
        pending, *values = lax.optimization_barrier((self.pending, *values))
        self.held.append((pending, self.first))
        half = self.size // 2
        bit = (self.plane.part >> (self.plane.bits - 1 - self.step)) & 1
        leave, *values = lax.optimization_barrier((self.total(self.first + (1 - bit) * half, half), *values))
        self.first, self.size = self.first + bit * half, half
        self.pending = self.plane.stage(leave, self.step)
        self.step += 1
        return values

    def finish(self, *values):
        while self.step < self.plane.bits:
            values = self.advance(*values)
        pending, *values = lax.optimization_barrier((self.pending, *values))
        self.held.append((pending, self.first))
        return self.total(self.first, self.size), *values

    def spread(self, mine):
        parts = lax.all_gather(mine, "seq")
        turned = jnp.stack([parts[i] for i in self.plane.reversed])
        return jnp.where(self.plane.core == 0, turned, parts).reshape(self.rows, self.width)


def scatter_rows(terms):
    return lax.psum_scatter(terms, "batch", scatter_dimension=0, tiled=True)


def local(
    tokens,
    cotangent,
    segment_ids,
    positions,
    attn_gain,
    qkv_weight,
    out_weight,
    mlp_gain,
    gate_up_weight,
    down_weight,
):
    seq = lax.axis_size("seq")
    chips = lax.axis_size("batch") // 2
    bits = seq.bit_length() - 1
    s = lax.axis_index("seq")
    swap = [(i, i ^ 1) for i in range(seq)]
    model_width = tokens.shape[2]
    rows = tokens.shape[1]
    if rows * 2 != DOC_MAX:
        raise ValueError("token shard")
    share = H // KV
    kv_width = KV * HD
    scale_factor = HD ** (-0.5)
    ff_width = gate_up_weight.shape[1] // 2

    shards = (qkv_weight, out_weight, gate_up_weight, down_weight)
    cuts = (2, 2, 8, max(1, min(4, model_width // (seq * 128))))
    units = sum((parts_of(i, one.shape[1], n) for i, (one, n) in enumerate(zip(shards, cuts))), ())
    qkv_whole, out_whole, gate_up_whole, down_whole = gathered(shards, chips, bits, units, 3)

    inputs = tokens[0].astype(F32)
    normed, inv_first = rms_parts(inputs, attn_gain)
    normed_low = normed.astype(BF16)
    projected = dot(normed_low, qkv_whole)

    row_start = s * rows
    own_segments = lax.dynamic_slice_in_dim(segment_ids[0], row_start, rows, 0)
    other = s ^ 1
    other_segments = lax.dynamic_slice_in_dim(segment_ids[0], other * rows, rows, 0)
    own_positions = lax.dynamic_slice_in_dim(positions[0], row_start, rows, 0)
    cosine, sine_part = rotary_tables(own_positions, HD)
    queries = projected[:, :model_width].astype(BF16).reshape(rows, H, HD)
    queries_rot = rotate(queries.astype(F32), cosine, sine_part).astype(BF16)
    queries_rot = queries_rot.reshape(rows, KV, share, HD)
    keys = projected[:, model_width : model_width + kv_width].astype(BF16).reshape(rows, KV, HD)
    keys_rot = rotate(keys.astype(F32), cosine, sine_part).astype(BF16).reshape(rows, kv_width)
    values = projected[:, model_width + kv_width :].astype(BF16)
    own_kv = jnp.concatenate([keys_rot, values], axis=1)
    other_kv = lax.ppermute(own_kv, "seq", swap)
    both_kv = jnp.concatenate([own_kv, other_kv], axis=0)
    all_keys = both_kv[:, :kv_width].reshape(2 * rows, KV, HD)
    all_values = both_kv[:, kv_width:].reshape(2 * rows, KV, HD)
    index = jnp.arange(rows, dtype=jnp.int32)
    allowed = jnp.concatenate(
        [
            (index[None, :] <= index[:, None]) & (own_segments[None, :] == own_segments[:, None]),
            (other < s) & (other_segments[None, :] == own_segments[:, None]),
        ],
        axis=1,
    )
    scores = (
        jnp.einsum("qgsd,kgd->gsqk", queries_rot, all_keys, preferred_element_type=F32)
        * scale_factor
    )
    masked = jnp.where(allowed[None, None], scores, -1e30)
    row_max = jnp.max(masked, axis=-1, keepdims=True)
    exps = jnp.exp(masked - row_max)
    probs = exps / jnp.sum(exps, axis=-1, keepdims=True)
    probs_low = probs.astype(BF16)
    attended = jnp.einsum("gsqk,kgd->qgsd", probs_low, all_values, preferred_element_type=F32)
    attended = attended.astype(BF16).reshape(rows, model_width)
    residual = inputs + dot(attended, out_whole)
    normed_mlp, inv_second = rms_parts(residual, mlp_gain)
    normed_mlp_low = normed_mlp.astype(BF16)
    gate_up = dot(normed_mlp_low, gate_up_whole)
    gate_part = gate_up[:, :ff_width]
    up_part = gate_up[:, ff_width:]
    sigmoid_gate = jax.nn.sigmoid(gate_part)
    hidden_low = (gate_part * sigmoid_gate * up_part).astype(BF16)
    output = (residual + dot(hidden_low, down_whole)).astype(BF16)

    grad_out = cotangent[0].astype(F32)
    grad_down = cotangent[0]
    down_terms, grad_down = lax.optimization_barrier((dot_tn(hidden_low, grad_down).astype(BF16), grad_down))
    down_fold = Fold(down_terms)
    grad_hidden = dot_nt(grad_down, down_whole)
    grad_gate = grad_hidden * up_part * sigmoid_gate * (1.0 + gate_part * (1.0 - sigmoid_gate))
    grad_up = grad_hidden * gate_part * sigmoid_gate
    grad_gate, grad_up = down_fold.advance(grad_gate.astype(BF16), grad_up.astype(BF16))
    grad_gate_up = jnp.concatenate([grad_gate, grad_up], axis=1)
    grad_normed_mlp = dot_nt(grad_gate_up, gate_up_whole)
    mlp_term = jnp.sum(grad_normed_mlp * residual * inv_second, axis=0)
    grad_resid = grad_out + norm_back(grad_normed_mlp, residual, inv_second, mlp_gain)
    grad_proj = grad_resid.astype(BF16)
    out_part = scatter_rows(dot_tn(attended, grad_proj).astype(BF16))
    grad_heads = dot_nt(grad_proj, out_whole)
    grad_heads = grad_heads.astype(BF16).reshape(rows, KV, share, HD)

    grad_probs = jnp.einsum("qgsd,kgd->gsqk", grad_heads, all_values, preferred_element_type=F32)
    inner_sum = jnp.sum(probs * grad_probs, axis=-1, keepdims=True)
    grad_scores = (probs * (grad_probs - inner_sum)).astype(BF16)
    grad_queries = (
        jnp.einsum("gsqk,kgd->qgsd", grad_scores, all_keys, preferred_element_type=F32)
        * scale_factor
    )
    grad_keys = (
        jnp.einsum("gsqk,qgsd->kgd", grad_scores, queries_rot, preferred_element_type=F32)
        * scale_factor
    )
    grad_values = jnp.einsum("gsqk,qgsd->kgd", probs_low, grad_heads, preferred_element_type=F32)
    grad_kv = jnp.concatenate(
        [grad_keys.reshape(2 * rows, kv_width), grad_values.reshape(2 * rows, kv_width)], axis=1
    )
    away = grad_kv[rows:].astype(BF16)
    arrived = lax.ppermute(away, "seq", swap)
    own_grad_kv = grad_kv[:rows] + arrived.astype(F32)
    back_queries = rotate(grad_queries.reshape(rows, H, HD), cosine, -sine_part)
    back_keys = rotate(own_grad_kv[:, :kv_width].reshape(rows, KV, HD), cosine, -sine_part)
    grad_qkv = jnp.concatenate(
        [
            back_queries.reshape(rows, model_width),
            back_keys.reshape(rows, kv_width),
            own_grad_kv[:, kv_width:],
        ],
        axis=1,
    ).astype(BF16)
    if down_fold.step < bits:
        (grad_qkv,) = down_fold.advance(grad_qkv)
    qkv_terms = dot_tn(normed_low, grad_qkv).astype(BF16)
    grad_normed = dot_nt(grad_qkv, qkv_whole)
    attn_term = jnp.sum(grad_normed * inputs * inv_first, axis=0)
    tokens_grad = (grad_resid + norm_back(grad_normed, inputs, inv_first, attn_gain)).astype(BF16)
    gains = jnp.concatenate([attn_term, mlp_term]).reshape(-1, 128)
    normed_mlp_low, gains = lax.optimization_barrier((normed_mlp_low, gains))
    gate_up_terms = dot_tn(normed_mlp_low, grad_gate_up).astype(BF16)
    out_grad = lax.psum(out_part, "seq")
    down_part, gate_up_terms = down_fold.finish(gate_up_terms)
    groups = [list(range(core, 2 * chips, 2)) for core in range(2)]
    down_part = lax.psum_scatter(down_part, "batch", scatter_dimension=0, axis_index_groups=groups)
    gate_up_grad, qkv_grad, gains = reduced((gate_up_terms, qkv_terms), gains, chips, bits, 512)
    gains = gains.reshape(-1)
    gate_up_grad, down_part = lax.optimization_barrier((gate_up_grad, down_part))
    down_grad = down_fold.spread(down_part)
    return (
        output[None],
        tokens_grad[None],
        gains[:model_width],
        qkv_grad.astype(F32),
        out_grad.astype(F32),
        gains[model_width:],
        gate_up_grad.astype(F32),
        down_grad.astype(F32),
    )


def solution(mesh):
    return jax.shard_map(
        local,
        mesh=mesh,
        in_specs=(
            P("batch", "seq", None),
            P("batch", "seq", None),
            P("batch", None),
            P("batch", None),
            P(),
            P("batch", None),
            P("batch", None),
            P(),
            P("batch", None),
            P("batch", None),
        ),
        out_specs=(
            P("batch", "seq", None),
            P("batch", "seq", None),
            P(),
            P("batch", None),
            P("batch", None),
            P(),
            P("batch", None),
            P("batch", None),
        ),
        check_vma=False,
    )
```

```python
import functools

import jax
import jax.numpy as jnp
from jax import lax
from jax.experimental import pallas as pl
from jax.experimental.pallas import tpu as pltpu
from jax.sharding import PartitionSpec as P

H = 32
KV = 4
HD = 64
DOC_MAX = 512
F32 = jnp.float32
BF16 = jnp.bfloat16


def rms_parts(values, gain_vector):
    inv_rms = lax.rsqrt(jnp.mean(values * values, axis=-1, keepdims=True) + 1e-05)
    return (values * inv_rms * gain_vector, inv_rms)


def norm_back(grad_normed, values, inv_rms, gain_vector):
    weighted = grad_normed * gain_vector
    inner_sum = jnp.mean(weighted * values, axis=-1, keepdims=True)
    return inv_rms * weighted - values * (inv_rms * inv_rms * inv_rms) * inner_sum


def rotary_tables(seq_positions, head_dim):
    half_dim = head_dim // 2
    frequency = 10000.0 ** (-jnp.arange(half_dim, dtype=F32) * 2.0 / head_dim)
    angles = seq_positions.astype(F32)[:, None] * frequency[None, :]
    return (jnp.cos(angles)[:, None, :], jnp.sin(angles)[:, None, :])


def rotate(values, cosine, sine_part):
    half_dim = values.shape[-1] // 2
    first_half = values[..., :half_dim]
    second_half = values[..., half_dim:]
    return jnp.concatenate(
        [
            first_half * cosine - second_half * sine_part,
            second_half * cosine + first_half * sine_part,
        ],
        axis=-1,
    )


def dot(left, right):
    return jnp.dot(left, right, preferred_element_type=F32)


def dot_nt(left, right):
    return lax.dot_general(left, right, (((1,), (1,)), ((), ())), preferred_element_type=F32)


def dot_tn(left, right):
    return lax.dot_general(left, right, (((0,), (0,)), ((), ())), preferred_element_type=F32)


class Place:
    def __init__(self, chips, bits):
        self.chips, self.bits = chips, bits
        self.s = lax.axis_index("seq")
        place = lax.axis_index("batch")
        self.z, self.core = place // 2, place % 2
        reverse = 0
        for bit in range(bits):
            reverse = reverse + ((self.s // (1 << bit)) % 2) * (1 << (bits - 1 - bit))
        self.part = reverse + self.core * (self.s - reverse)

    def sibling(self):
        return {"batch": self.z * 2 + 1 - self.core}

    def chip(self, shift):
        return {"batch": ((self.z + shift) % self.chips) * 2 + self.core}

    def partner(self, step):
        first, second = 1 << step, 1 << (self.bits - 1 - step)
        mask = first + self.core * (second - first)
        return {"seq": self.s + mask * (1 - 2 * ((self.s // mask) % 2))}

    def fellows(self):
        found = [self.sibling()] + [self.partner(step) for step in range(self.bits)]
        step = 1
        while step < self.chips:
            found.append({"batch": (self.z + step * (1 - 2 * ((self.z // step) % 2))) * 2 + self.core})
            step *= 2
        return found

    def bit(self, step):
        return (self.part // (1 << (self.bits - 1 - step))) % 2

    def part_of(self, subset):
        part = self.part
        for step in range(self.bits):
            if subset >> step & 1:
                weight = 1 << (self.bits - 1 - step)
                part = part + weight * (1 - 2 * self.bit(step))
        return part


def reduce_kernel(chips, bits, count, terms, small, out, arrived, small_out, *scratch):
    halves = scratch[:bits]
    own, got, along, final = scratch[bits : bits + 4]
    (own_sem, got_sem, core_out, core_in, half_out, half_in, along_out, along_in, spread_out, spread_in, local_sem) = (
        scratch[bits + 4 : -4]
    )
    small_sum, small_got, small_send, small_recv = scratch[-4:]
    here = Place(chips, bits)
    rows, width = own.shape[2], own.shape[3]
    piece = rows >> bits
    slots = own.shape[0]
    seq = 1 << bits

    barrier = pltpu.get_barrier_semaphore()
    peers = [here.sibling()] + [here.partner(i) for i in range(bits)] + [here.chip(k) for k in range(1, chips)]
    fellows = here.fellows()
    for peer in peers:
        pl.semaphore_signal(barrier, inc=1, device_id=peer, device_id_type=pl.DeviceIdType.MESH)
    pl.semaphore_wait(barrier, len(peers))

    def columns(j):
        return pl.ds(pl.multiple_of(j * width, 128), width)

    def core_copy(j):
        return pltpu.make_async_remote_copy(
            src_ref=terms.at[:, 1 - here.core, :, columns(j)],
            dst_ref=arrived.at[j],
            send_sem=core_out.at[j],
            recv_sem=core_in.at[j],
            device_id=here.sibling(),
            device_id_type=pl.DeviceIdType.MESH,
        )

    def own_load(j):
        return pltpu.make_async_copy(terms.at[:, here.core, :, columns(j)], own.at[j % slots], own_sem.at[j])

    def got_load(j):
        return pltpu.make_async_copy(arrived.at[j], got.at[j % 2], got_sem.at[j])

    def offset(step):
        total = 0
        for i in range(step):
            total = total + here.bit(i) * (rows >> (i + 1))
        return total

    def half_copy(j, step):
        half = rows >> (step + 1)
        first = pl.multiple_of(offset(step) + (1 - here.bit(step)) * half, piece)
        return pltpu.make_async_remote_copy(
            src_ref=own.at[j % slots, :, pl.ds(first, half), :],
            dst_ref=halves[step].at[j],
            send_sem=half_out.at[j, step],
            recv_sem=half_in.at[j, step],
            device_id=here.partner(step),
            device_id_type=pl.DeviceIdType.MESH,
        )

    def along_copy(j, k):
        first = pl.multiple_of(offset(bits), piece)
        return pltpu.make_async_remote_copy(
            src_ref=own.at[j % slots, (here.z + k) % chips, pl.ds(first, piece), :],
            dst_ref=along.at[j, k - 1],
            send_sem=along_out.at[j, k - 1],
            recv_sem=along_in.at[j, k - 1],
            device_id=here.chip(k),
            device_id_type=pl.DeviceIdType.MESH,
        )

    def place_of(j, subset):
        return out.at[pl.ds(pl.multiple_of(here.part_of(subset) * piece, piece), piece), columns(j)]

    def spread_copy(j, subset):
        last = subset.bit_length() - 1
        parent = subset ^ (1 << last)
        return pltpu.make_async_remote_copy(
            src_ref=final.at[j] if parent == 0 else place_of(j, parent),
            dst_ref=place_of(j, parent),
            send_sem=spread_out.at[j, subset - 1],
            recv_sem=spread_in.at[j, subset - 1],
            device_id=here.partner(last),
            device_id_type=pl.DeviceIdType.MESH,
        )

    def local_copy(j):
        return pltpu.make_async_copy(final.at[j], place_of(j, 0), local_sem.at[j])

    def level(size):
        return [subset for subset in range(1, seq) if bin(subset).count("1") == size]

    def fresh(j):
        core_copy(j).start()

    def loads(j):
        core_copy(j).wait()
        own_load(j).start()
        got_load(j).start()

    def first_sum(j):
        own_load(j).wait()
        got_load(j).wait()
        block = 32 if rows % 32 == 0 else 16
        blocks = rows // block
        slot = j % slots

        def body(index, carry):
            z = index // blocks
            span = pl.ds(pl.multiple_of((index % blocks) * block, block), block)
            own[slot, z, span, :] = (
                own[slot, z, span, :].astype(F32) + got[j % 2, z, span, :].astype(F32)
            ).astype(BF16)
            return carry

        lax.fori_loop(0, chips * blocks, body, 0)

    def half_sum(j, step):
        half_copy(j, step).wait()
        half = rows >> (step + 1)
        block = 32 if half % 32 == 0 else 16
        blocks = half // block
        slot = j % slots
        start = offset(step + 1)

        def body(index, carry):
            z = index // blocks
            first = (index % blocks) * block
            there = pl.ds(pl.multiple_of(first, block), block)
            span = pl.ds(pl.multiple_of(start + first, block), block)
            own[slot, z, span, :] = (
                own[slot, z, span, :].astype(F32) + halves[step][j, z, there, :].astype(F32)
            ).astype(BF16)
            return carry

        lax.fori_loop(0, chips * blocks, body, 0)

    def send_along(j):
        for k in range(1, chips):
            along_copy(j, k).start()

    def last_sum(j):
        for k in range(1, chips):
            along_copy(j, k).wait()
        block = 16
        slot = j % slots
        start = offset(bits)

        def body(index, carry):
            first = index * block
            there = pl.ds(pl.multiple_of(first, block), block)
            total = own[slot, here.z, pl.ds(pl.multiple_of(start + first, block), block), :].astype(F32)
            for k in range(chips - 1):
                total = total + along[j, k, there, :].astype(F32)
            final[j, there, :] = total.astype(BF16)
            return carry

        lax.fori_loop(0, piece // block, body, 0)
        local_copy(j).start()
        for subset in level(1):
            spread_copy(j, subset).start()

    def pass_on(j, size):
        for subset in level(size):
            spread_copy(j, subset).wait()
        for subset in level(size + 1):
            spread_copy(j, subset).start()

    def small_copy(step):
        return pltpu.make_async_remote_copy(
            src_ref=small_sum.at[step],
            dst_ref=small_got.at[step],
            send_sem=small_send.at[step],
            recv_sem=small_recv.at[step],
            device_id=fellows[step],
            device_id_type=pl.DeviceIdType.MESH,
        )

    def small_step(step):
        if step:
            small_copy(step - 1).wait()
            small_sum[step] = small_sum[step - 1] + small_got[step - 1]
        if step < len(fellows):
            small_copy(step).start()
        else:
            small_out[...] = small_sum[step]

    stages = [fresh, loads, first_sum, lambda j: half_copy(j, 0).start()]
    for step in range(bits):

        def stage(j, step=step):
            half_sum(j, step)
            if step + 1 < bits:
                half_copy(j, step + 1).start()
            else:
                send_along(j)

        stages.append(stage)
    stages.append(last_sum)
    for size in range(1, bits + 1):
        stages.append(lambda j, size=size: pass_on(j, size))
    stages.append(lambda j: local_copy(j).wait())
    order = list(range(3, len(stages))) + [2, 1, 0]

    def round_of(now, carry):
        for step in range(len(fellows) + 1):

            @pl.when(now == step)
            def _(step=step):
                small_step(step)

        for number in order:
            chunk = now - number

            @pl.when((chunk >= 0) & (chunk < count))
            def _(number=number, chunk=chunk):
                stages[number](chunk)

        return carry

    small_sum[0] = small[...]
    lax.fori_loop(0, count + len(stages) - 1, round_of, 0)


def reduced(terms, small, chips, bits, count, number):
    rows, width = terms.shape[0] // (2 * chips), terms.shape[1]
    seq, wide = 1 << bits, width // count
    piece = rows // seq
    slots = bits + 5
    dma = pltpu.SemaphoreType.DMA
    steps = 1 + bits + (chips - 1).bit_length()
    out, _, small_out = pl.pallas_call(
        functools.partial(reduce_kernel, chips, bits, count),
        out_shape=(
            jax.ShapeDtypeStruct((rows, width), BF16),
            jax.ShapeDtypeStruct((count, chips, rows, wide), BF16),
            jax.ShapeDtypeStruct(small.shape, F32),
        ),
        in_specs=[pl.BlockSpec(memory_space=pl.ANY), pl.BlockSpec(memory_space=pltpu.VMEM)],
        out_specs=(
            pl.BlockSpec(memory_space=pl.ANY),
            pl.BlockSpec(memory_space=pl.ANY),
            pl.BlockSpec(memory_space=pltpu.VMEM),
        ),
        scratch_shapes=[pltpu.VMEM((count, chips, rows >> (step + 1), wide), BF16) for step in range(bits)]
        + [
            pltpu.VMEM((slots, chips, rows, wide), BF16),
            pltpu.VMEM((2, chips, rows, wide), BF16),
            pltpu.VMEM((count, chips - 1, piece, wide), BF16),
            pltpu.VMEM((count, piece, wide), BF16),
            dma((count,)),
            dma((count,)),
            dma((count,)),
            dma((count,)),
            dma((count, bits)),
            dma((count, bits)),
            dma((count, chips - 1)),
            dma((count, chips - 1)),
            dma((count, seq - 1)),
            dma((count, seq - 1)),
            dma((count,)),
            pltpu.VMEM((steps + 1,) + small.shape, F32),
            pltpu.VMEM((steps,) + small.shape, F32),
            dma((steps,)),
            dma((steps,)),
        ],
        compiler_params=pltpu.CompilerParams(
            collective_id=number, has_side_effects=True, vmem_limit_bytes=62 * 1024 * 1024
        ),
        cost_estimate=pl.CostEstimate(flops=0, bytes_accessed=800_000_000, transcendentals=0),
    )(terms.reshape(chips, 2, rows, width), small)
    return out, small_out


def gather_kernel(chips, bits, units, weights, ahead, *refs):
    shards, wholes = refs[:weights], refs[weights : 2 * weights]
    held = refs[2 * weights : 3 * weights]
    (in_sem, own_sem, along_out, along_in, spread_out, spread_in, turn_out, turn_in) = refs[3 * weights :]
    here = Place(chips, bits)
    seq = 1 << bits

    barrier = pltpu.get_barrier_semaphore()
    peers = [here.sibling()] + [here.partner(i) for i in range(bits)] + [here.chip(k) for k in range(1, chips)]
    for peer in peers:
        pl.semaphore_signal(barrier, inc=1, device_id=peer, device_id_type=pl.DeviceIdType.MESH)
    pl.semaphore_wait(barrier, len(peers))

    def rows_of(unit, shift):
        which, first, width = units[unit]
        count = shards[which].shape[0]
        row = (((here.z - shift) % chips) * 2 + here.core) * count
        return which, row, count, first, width

    def piece_of(unit, shift, subset):
        which, row, count, first, width = rows_of(unit, shift)
        part = here.part_of(subset)
        if (count // seq) % 16 == 0:
            size = count // seq
            return which, pl.ds(pl.multiple_of(row + part * size, 16), size), pl.ds(first, width)
        size = width // seq
        return which, pl.ds(pl.multiple_of(row, 16), count), pl.ds(pl.multiple_of(first + part * size, 128), size)

    def remote(source, target, sems, index, device):
        return pltpu.make_async_remote_copy(
            src_ref=source,
            dst_ref=target,
            send_sem=sems[0].at[index],
            recv_sem=sems[1].at[index],
            device_id=device,
            device_id_type=pl.DeviceIdType.MESH,
        )

    def along(unit, k):
        which, row, count, first, width = rows_of(unit, 0)
        _, there, columns = piece_of(unit, 0, 0)
        part = here.part
        if (count // seq) % 16 == 0:
            size = count // seq
            source = shards[which].at[pl.ds(pl.multiple_of(part * size, 16), size), columns]
        else:
            source = shards[which].at[:, columns]
        return remote(source, wholes[which].at[there, columns], (along_out, along_in), (unit, k - 1), here.chip(k))

    def spread(unit, k, subset):
        last = subset.bit_length() - 1
        which, there, columns = piece_of(unit, k, subset ^ (1 << last))
        region = wholes[which].at[there, columns]
        return remote(region, region, (spread_out, spread_in), (unit, k - 1, subset - 1), here.partner(last))

    def turn(unit, k):
        which, row, count, first, width = rows_of(unit, k)
        there = pl.ds(pl.multiple_of(row, 16), count)
        region = wholes[which].at[there, pl.ds(first, width)]
        source = region if k else shards[which].at[:, pl.ds(first, width)]
        return remote(source, region, (turn_out, turn_in), (unit, k), here.sibling())

    def load(which):
        return pltpu.make_async_copy(shards[which], held[which], in_sem.at[which])

    def store(which):
        count = shards[which].shape[0]
        row = (here.z * 2 + here.core) * count
        there = pl.ds(pl.multiple_of(row, 16), count)
        return pltpu.make_async_copy(held[which], wholes[which].at[there], own_sem.at[which])

    def level(size):
        return [subset for subset in range(1, seq) if bin(subset).count("1") == size]

    shifts = range(1, chips)

    def begin(unit):
        for k in shifts:
            along(unit, k).start()
        turn(unit, 0).start()

    def arrive(unit):
        for k in shifts:
            along(unit, k).wait()
            for subset in level(1):
                spread(unit, k, subset).start()

    def pass_on(unit, size):
        for k in shifts:
            for subset in level(size):
                spread(unit, k, subset).wait()
            for subset in level(size + 1):
                spread(unit, k, subset).start()
            if size == bits:
                turn(unit, k).start()

    def finish(unit):
        for k in range(chips):
            turn(unit, k).wait()

    for which in range(weights):
        load(which).start()
    stages = [arrive]
    for size in range(1, bits + 1):
        stages.append(lambda unit, size=size: pass_on(unit, size))
    stages.append(finish)
    for unit in range(min(ahead, len(units))):
        begin(unit)
    for now in range(len(units) + len(stages) - 1):
        if now + ahead < len(units):
            begin(now + ahead)
        for number, stage in enumerate(stages):
            unit = now - number
            if 0 <= unit < len(units):
                stage(unit)
        if now < weights:
            load(now).wait()
            store(now).start()
    for which in range(weights):
        if which >= len(units) + len(stages) - 1:
            load(which).wait()
            store(which).start()
    for which in range(weights):
        store(which).wait()


def gathered(shards, chips, bits, units, ahead):
    weights, seq, count = len(shards), 1 << bits, len(units)
    dma = pltpu.SemaphoreType.DMA
    return pl.pallas_call(
        functools.partial(gather_kernel, chips, bits, units, weights, ahead),
        out_shape=tuple(jax.ShapeDtypeStruct((2 * chips * one.shape[0], one.shape[1]), one.dtype) for one in shards),
        in_specs=[pl.BlockSpec(memory_space=pl.ANY)] * weights,
        out_specs=tuple(pl.BlockSpec(memory_space=pl.ANY) for _ in shards),
        scratch_shapes=[pltpu.VMEM(one.shape, one.dtype) for one in shards]
        + [
            dma((weights,)),
            dma((weights,)),
            dma((count, chips - 1)),
            dma((count, chips - 1)),
            dma((count, chips - 1, seq - 1)),
            dma((count, chips - 1, seq - 1)),
            dma((count, chips)),
            dma((count, chips)),
        ],
        compiler_params=pltpu.CompilerParams(
            collective_id=1, has_side_effects=True, vmem_limit_bytes=62 * 1024 * 1024
        ),
        cost_estimate=pl.CostEstimate(flops=0, bytes_accessed=900_000_000, transcendentals=0),
    )(*shards)


def parts_of(which, width, count):
    return tuple((which, i * (width // count), width // count) for i in range(count))


def scatter_rows(terms):
    return lax.psum_scatter(terms, "batch", scatter_dimension=0, tiled=True)


def local(
    tokens,
    cotangent,
    segment_ids,
    positions,
    attn_gain,
    qkv_weight,
    out_weight,
    mlp_gain,
    gate_up_weight,
    down_weight,
):
    seq = lax.axis_size("seq")
    chips = lax.axis_size("batch") // 2
    bits = seq.bit_length() - 1
    s = lax.axis_index("seq")
    swap = [(i, i ^ 1) for i in range(seq)]
    model_width = tokens.shape[2]
    rows = tokens.shape[1]
    if rows * 2 != DOC_MAX:
        raise ValueError("token shard")
    share = H // KV
    kv_width = KV * HD
    scale_factor = HD ** (-0.5)
    ff_width = gate_up_weight.shape[1] // 2

    shards = (qkv_weight, out_weight, gate_up_weight, down_weight)
    cuts = (2, 2, 8, max(1, min(4, model_width // (seq * 128))))
    units = sum((parts_of(i, one.shape[1], n) for i, (one, n) in enumerate(zip(shards, cuts))), ())
    qkv_whole, out_whole, gate_up_whole, down_whole = gathered(shards, chips, bits, units, 3)

    inputs = tokens[0].astype(F32)
    normed, inv_first = rms_parts(inputs, attn_gain)
    normed_low = normed.astype(BF16)
    projected = dot(normed_low, qkv_whole)

    row_start = s * rows
    own_segments = lax.dynamic_slice_in_dim(segment_ids[0], row_start, rows, 0)
    other = s ^ 1
    other_segments = lax.dynamic_slice_in_dim(segment_ids[0], other * rows, rows, 0)
    own_positions = lax.dynamic_slice_in_dim(positions[0], row_start, rows, 0)
    cosine, sine_part = rotary_tables(own_positions, HD)
    queries = projected[:, :model_width].astype(BF16).reshape(rows, H, HD)
    queries_rot = rotate(queries.astype(F32), cosine, sine_part).astype(BF16)
    queries_rot = queries_rot.reshape(rows, KV, share, HD)
    keys = projected[:, model_width : model_width + kv_width].astype(BF16).reshape(rows, KV, HD)
    keys_rot = rotate(keys.astype(F32), cosine, sine_part).astype(BF16).reshape(rows, kv_width)
    values = projected[:, model_width + kv_width :].astype(BF16)
    own_kv = jnp.concatenate([keys_rot, values], axis=1)
    other_kv = lax.ppermute(own_kv, "seq", swap)
    both_kv = jnp.concatenate([own_kv, other_kv], axis=0)
    all_keys = both_kv[:, :kv_width].reshape(2 * rows, KV, HD)
    all_values = both_kv[:, kv_width:].reshape(2 * rows, KV, HD)
    index = jnp.arange(rows, dtype=jnp.int32)
    allowed = jnp.concatenate(
        [
            (index[None, :] <= index[:, None]) & (own_segments[None, :] == own_segments[:, None]),
            (other < s) & (other_segments[None, :] == own_segments[:, None]),
        ],
        axis=1,
    )
    scores = (
        jnp.einsum("qgsd,kgd->gsqk", queries_rot, all_keys, preferred_element_type=F32)
        * scale_factor
    )
    masked = jnp.where(allowed[None, None], scores, -1e30)
    row_max = jnp.max(masked, axis=-1, keepdims=True)
    exps = jnp.exp(masked - row_max)
    probs = exps / jnp.sum(exps, axis=-1, keepdims=True)
    probs_low = probs.astype(BF16)
    attended = jnp.einsum("gsqk,kgd->qgsd", probs_low, all_values, preferred_element_type=F32)
    attended = attended.astype(BF16).reshape(rows, model_width)
    residual = inputs + dot(attended, out_whole)
    normed_mlp, inv_second = rms_parts(residual, mlp_gain)
    normed_mlp_low = normed_mlp.astype(BF16)
    gate_up = dot(normed_mlp_low, gate_up_whole)
    gate_part = gate_up[:, :ff_width]
    up_part = gate_up[:, ff_width:]
    sigmoid_gate = jax.nn.sigmoid(gate_part)
    hidden_low = (gate_part * sigmoid_gate * up_part).astype(BF16)

    grad_out = cotangent[0].astype(F32)
    grad_down = cotangent[0]
    early = model_width * 4 // 8
    early_terms = dot_tn(hidden_low, grad_down[:, :early]).astype(BF16)
    early_terms, grad_down = lax.optimization_barrier((early_terms, grad_down))
    down_early = scatter_rows(early_terms)
    down_terms = dot_tn(hidden_low, grad_down[:, early:]).astype(BF16)
    grad_hidden = dot_nt(grad_down, down_whole)
    grad_gate = grad_hidden * up_part * sigmoid_gate * (1.0 + gate_part * (1.0 - sigmoid_gate))
    grad_up = grad_hidden * gate_part * sigmoid_gate
    grad_gate_up = jnp.concatenate([grad_gate, grad_up], axis=1).astype(BF16)
    gate_up_terms = dot_tn(normed_mlp_low, grad_gate_up).astype(BF16)
    grad_normed_mlp = dot_nt(grad_gate_up, gate_up_whole)
    mlp_term = jnp.sum(grad_normed_mlp * residual * inv_second, axis=0)
    grad_resid = grad_out + norm_back(grad_normed_mlp, residual, inv_second, mlp_gain)
    grad_proj = grad_resid.astype(BF16)
    out_part = scatter_rows(dot_tn(attended, grad_proj).astype(BF16))
    grad_heads = dot_nt(grad_proj, out_whole)
    grad_heads = grad_heads.astype(BF16).reshape(rows, KV, share, HD)

    grad_probs = jnp.einsum("qgsd,kgd->gsqk", grad_heads, all_values, preferred_element_type=F32)
    inner_sum = jnp.sum(probs * grad_probs, axis=-1, keepdims=True)
    grad_scores = (probs * (grad_probs - inner_sum)).astype(BF16)
    grad_queries = (
        jnp.einsum("gsqk,kgd->qgsd", grad_scores, all_keys, preferred_element_type=F32)
        * scale_factor
    )
    grad_keys = (
        jnp.einsum("gsqk,qgsd->kgd", grad_scores, queries_rot, preferred_element_type=F32)
        * scale_factor
    )
    grad_values = jnp.einsum("gsqk,qgsd->kgd", probs_low, grad_heads, preferred_element_type=F32)
    grad_kv = jnp.concatenate(
        [grad_keys.reshape(2 * rows, kv_width), grad_values.reshape(2 * rows, kv_width)], axis=1
    )
    away = grad_kv[rows:].astype(BF16)
    arrived = lax.ppermute(away, "seq", swap)
    own_grad_kv = grad_kv[:rows] + arrived.astype(F32)
    back_queries = rotate(grad_queries.reshape(rows, H, HD), cosine, -sine_part)
    back_keys = rotate(own_grad_kv[:, :kv_width].reshape(rows, KV, HD), cosine, -sine_part)
    grad_qkv = jnp.concatenate(
        [
            back_queries.reshape(rows, model_width),
            back_keys.reshape(rows, kv_width),
            own_grad_kv[:, kv_width:],
        ],
        axis=1,
    ).astype(BF16)
    qkv_terms = dot_tn(normed_low, grad_qkv).astype(BF16)
    qkv_part = scatter_rows(qkv_terms)
    grad_normed = dot_nt(grad_qkv, qkv_whole)
    attn_term = jnp.sum(grad_normed * inputs * inv_first, axis=0)
    tokens_grad = (grad_resid + norm_back(grad_normed, inputs, inv_first, attn_gain)).astype(BF16)
    gains = jnp.concatenate([attn_term, mlp_term]).reshape(-1, 128)
    gains, down_early = lax.optimization_barrier((gains, down_early))
    gate_up_grad, gains = reduced(gate_up_terms, gains, chips, bits, 11, 0)
    gains = gains.reshape(-1)
    gate_up_grad, down_early, out_part, qkv_part, down_terms = lax.optimization_barrier(
        (gate_up_grad, down_early, out_part, qkv_part, down_terms)
    )
    if down_weight.shape[0] // seq % 16 == 0:
        down_late, _ = reduced(down_terms, jnp.zeros((8, 128), F32), chips, bits, 4, 2)
    else:
        down_late = lax.psum(scatter_rows(down_terms), "seq")
    down_late, gate_up_grad, hidden_low = lax.optimization_barrier((down_late, gate_up_grad, hidden_low))
    output = (residual + dot(hidden_low, down_whole)).astype(BF16)
    down_early, out_grad, qkv_grad = lax.psum((down_early, out_part, qkv_part), "seq")
    down_grad = jnp.concatenate([down_early, down_late], axis=1)
    return (
        output[None],
        tokens_grad[None],
        gains[:model_width],
        qkv_grad.astype(F32),
        out_grad.astype(F32),
        gains[model_width:],
        gate_up_grad.astype(F32),
        down_grad.astype(F32),
    )


def solution(mesh):
    return jax.shard_map(
        local,
        mesh=mesh,
        in_specs=(
            P("batch", "seq", None),
            P("batch", "seq", None),
            P("batch", None),
            P("batch", None),
            P(),
            P("batch", None),
            P("batch", None),
            P(),
            P("batch", None),
            P("batch", None),
        ),
        out_specs=(
            P("batch", "seq", None),
            P("batch", "seq", None),
            P(),
            P("batch", None),
            P("batch", None),
            P(),
            P("batch", None),
            P("batch", None),
        ),
        check_vma=False,
    )
```

```python
import functools

import jax
import jax.numpy as jnp
from jax import lax
from jax.experimental import pallas as pl
from jax.experimental.pallas import tpu as pltpu
from jax.sharding import PartitionSpec as P

H = 32
KV = 4
HD = 64
DOC_MAX = 512
F32 = jnp.float32
BF16 = jnp.bfloat16


def rms_parts(values, gain_vector):
    inv_rms = lax.rsqrt(jnp.mean(values * values, axis=-1, keepdims=True) + 1e-05)
    return (values * inv_rms * gain_vector, inv_rms)


def norm_back(grad_normed, values, inv_rms, gain_vector):
    weighted = grad_normed * gain_vector
    inner_sum = jnp.mean(weighted * values, axis=-1, keepdims=True)
    return inv_rms * weighted - values * (inv_rms * inv_rms * inv_rms) * inner_sum


def rotary_tables(seq_positions, head_dim):
    half_dim = head_dim // 2
    frequency = 10000.0 ** (-jnp.arange(half_dim, dtype=F32) * 2.0 / head_dim)
    angles = seq_positions.astype(F32)[:, None] * frequency[None, :]
    return (jnp.cos(angles)[:, None, :], jnp.sin(angles)[:, None, :])


def rotate(values, cosine, sine_part):
    half_dim = values.shape[-1] // 2
    first_half = values[..., :half_dim]
    second_half = values[..., half_dim:]
    return jnp.concatenate(
        [
            first_half * cosine - second_half * sine_part,
            second_half * cosine + first_half * sine_part,
        ],
        axis=-1,
    )


def dot(left, right):
    return jnp.dot(left, right, preferred_element_type=F32)


def dot_nt(left, right):
    return lax.dot_general(left, right, (((1,), (1,)), ((), ())), preferred_element_type=F32)


def dot_tn(left, right):
    return lax.dot_general(left, right, (((0,), (0,)), ((), ())), preferred_element_type=F32)


class Place:
    def __init__(self, chips, bits):
        self.chips, self.bits = chips, bits
        self.s = lax.axis_index("seq")
        place = lax.axis_index("batch")
        self.z, self.core = place // 2, place % 2
        reverse = 0
        for bit in range(bits):
            reverse = reverse + ((self.s // (1 << bit)) % 2) * (1 << (bits - 1 - bit))
        self.part = reverse + self.core * (self.s - reverse)

    def sibling(self):
        return {"batch": self.z * 2 + 1 - self.core}

    def chip(self, shift):
        return {"batch": ((self.z + shift) % self.chips) * 2 + self.core}

    def partner(self, step):
        first, second = 1 << step, 1 << (self.bits - 1 - step)
        mask = first + self.core * (second - first)
        return {"seq": self.s + mask * (1 - 2 * ((self.s // mask) % 2))}

    def fellows(self):
        found = [self.sibling()] + [self.partner(step) for step in range(self.bits)]
        step = 1
        while step < self.chips:
            found.append({"batch": (self.z + step * (1 - 2 * ((self.z // step) % 2))) * 2 + self.core})
            step *= 2
        return found

    def bit(self, step):
        return (self.part // (1 << (self.bits - 1 - step))) % 2

    def part_of(self, subset):
        part = self.part
        for step in range(self.bits):
            if subset >> step & 1:
                weight = 1 << (self.bits - 1 - step)
                part = part + weight * (1 - 2 * self.bit(step))
        return part


def reduce_kernel(chips, bits, count, terms, small, out, arrived, small_out, *scratch):
    halves = scratch[:bits]
    own, got, along, final = scratch[bits : bits + 4]
    (own_sem, got_sem, core_out, core_in, half_out, half_in, along_out, along_in, spread_out, spread_in, local_sem) = (
        scratch[bits + 4 : -4]
    )
    small_sum, small_got, small_send, small_recv = scratch[-4:]
    here = Place(chips, bits)
    rows, width = own.shape[2], own.shape[3]
    piece = rows >> bits
    slots = own.shape[0]
    seq = 1 << bits

    barrier = pltpu.get_barrier_semaphore()
    peers = [here.sibling()] + [here.partner(i) for i in range(bits)] + [here.chip(k) for k in range(1, chips)]
    fellows = here.fellows()
    for peer in peers:
        pl.semaphore_signal(barrier, inc=1, device_id=peer, device_id_type=pl.DeviceIdType.MESH)
    pl.semaphore_wait(barrier, len(peers))

    def columns(j):
        return pl.ds(pl.multiple_of(j * width, 128), width)

    def core_copy(j):
        return pltpu.make_async_remote_copy(
            src_ref=terms.at[:, 1 - here.core, :, columns(j)],
            dst_ref=arrived.at[j],
            send_sem=core_out.at[j],
            recv_sem=core_in.at[j],
            device_id=here.sibling(),
            device_id_type=pl.DeviceIdType.MESH,
        )

    def own_load(j):
        return pltpu.make_async_copy(terms.at[:, here.core, :, columns(j)], own.at[j % slots], own_sem.at[j])

    def got_load(j):
        return pltpu.make_async_copy(arrived.at[j], got.at[j % 2], got_sem.at[j])

    def offset(step):
        total = 0
        for i in range(step):
            total = total + here.bit(i) * (rows >> (i + 1))
        return total

    def half_copy(j, step):
        half = rows >> (step + 1)
        first = pl.multiple_of(offset(step) + (1 - here.bit(step)) * half, piece)
        return pltpu.make_async_remote_copy(
            src_ref=own.at[j % slots, :, pl.ds(first, half), :],
            dst_ref=halves[step].at[j],
            send_sem=half_out.at[j, step],
            recv_sem=half_in.at[j, step],
            device_id=here.partner(step),
            device_id_type=pl.DeviceIdType.MESH,
        )

    def along_copy(j, k):
        first = pl.multiple_of(offset(bits), piece)
        return pltpu.make_async_remote_copy(
            src_ref=own.at[j % slots, (here.z + k) % chips, pl.ds(first, piece), :],
            dst_ref=along.at[j, k - 1],
            send_sem=along_out.at[j, k - 1],
            recv_sem=along_in.at[j, k - 1],
            device_id=here.chip(k),
            device_id_type=pl.DeviceIdType.MESH,
        )

    def place_of(j, subset):
        return out.at[pl.ds(pl.multiple_of(here.part_of(subset) * piece, piece), piece), columns(j)]

    def spread_copy(j, subset):
        last = subset.bit_length() - 1
        parent = subset ^ (1 << last)
        return pltpu.make_async_remote_copy(
            src_ref=final.at[j] if parent == 0 else place_of(j, parent),
            dst_ref=place_of(j, parent),
            send_sem=spread_out.at[j, subset - 1],
            recv_sem=spread_in.at[j, subset - 1],
            device_id=here.partner(last),
            device_id_type=pl.DeviceIdType.MESH,
        )

    def local_copy(j):
        return pltpu.make_async_copy(final.at[j], place_of(j, 0), local_sem.at[j])

    def level(size):
        return [subset for subset in range(1, seq) if bin(subset).count("1") == size]

    def fresh(j):
        core_copy(j).start()

    def loads(j):
        core_copy(j).wait()
        own_load(j).start()
        got_load(j).start()

    def first_sum(j):
        own_load(j).wait()
        got_load(j).wait()
        block = 32 if rows % 32 == 0 else 16
        blocks = rows // block
        slot = j % slots

        def body(index, carry):
            z = index // blocks
            span = pl.ds(pl.multiple_of((index % blocks) * block, block), block)
            own[slot, z, span, :] = (
                own[slot, z, span, :].astype(F32) + got[j % 2, z, span, :].astype(F32)
            ).astype(BF16)
            return carry

        lax.fori_loop(0, chips * blocks, body, 0)

    def half_sum(j, step):
        half_copy(j, step).wait()
        half = rows >> (step + 1)
        block = 32 if half % 32 == 0 else 16
        blocks = half // block
        slot = j % slots
        start = offset(step + 1)

        def body(index, carry):
            z = index // blocks
            first = (index % blocks) * block
            there = pl.ds(pl.multiple_of(first, block), block)
            span = pl.ds(pl.multiple_of(start + first, block), block)
            own[slot, z, span, :] = (
                own[slot, z, span, :].astype(F32) + halves[step][j, z, there, :].astype(F32)
            ).astype(BF16)
            return carry

        lax.fori_loop(0, chips * blocks, body, 0)

    def send_along(j):
        for k in range(1, chips):
            along_copy(j, k).start()

    def last_sum(j):
        for k in range(1, chips):
            along_copy(j, k).wait()
        block = 16
        slot = j % slots
        start = offset(bits)

        def body(index, carry):
            first = index * block
            there = pl.ds(pl.multiple_of(first, block), block)
            total = own[slot, here.z, pl.ds(pl.multiple_of(start + first, block), block), :].astype(F32)
            for k in range(chips - 1):
                total = total + along[j, k, there, :].astype(F32)
            final[j, there, :] = total.astype(BF16)
            return carry

        lax.fori_loop(0, piece // block, body, 0)
        local_copy(j).start()
        for subset in level(1):
            spread_copy(j, subset).start()

    def pass_on(j, size):
        for subset in level(size):
            spread_copy(j, subset).wait()
        for subset in level(size + 1):
            spread_copy(j, subset).start()

    def small_copy(step):
        return pltpu.make_async_remote_copy(
            src_ref=small_sum.at[step],
            dst_ref=small_got.at[step],
            send_sem=small_send.at[step],
            recv_sem=small_recv.at[step],
            device_id=fellows[step],
            device_id_type=pl.DeviceIdType.MESH,
        )

    def small_step(step):
        if step:
            small_copy(step - 1).wait()
            small_sum[step] = small_sum[step - 1] + small_got[step - 1]
        if step < len(fellows):
            small_copy(step).start()
        else:
            small_out[...] = small_sum[step]

    stages = [fresh, loads, first_sum, lambda j: half_copy(j, 0).start()]
    for step in range(bits):

        def stage(j, step=step):
            half_sum(j, step)
            if step + 1 < bits:
                half_copy(j, step + 1).start()
            else:
                send_along(j)

        stages.append(stage)
    stages.append(last_sum)
    for size in range(1, bits + 1):
        stages.append(lambda j, size=size: pass_on(j, size))
    stages.append(lambda j: local_copy(j).wait())
    order = list(range(3, len(stages))) + [2, 1, 0]

    def round_of(now, carry):
        for step in range(len(fellows) + 1):

            @pl.when(now == step)
            def _(step=step):
                small_step(step)

        for number in order:
            chunk = now - number

            @pl.when((chunk >= 0) & (chunk < count))
            def _(number=number, chunk=chunk):
                stages[number](chunk)

        return carry

    small_sum[0] = small[...]
    lax.fori_loop(0, count + len(stages) - 1, round_of, 0)


def reduced(terms, small, chips, bits, count, number):
    rows, width = terms.shape[0] // (2 * chips), terms.shape[1]
    seq, wide = 1 << bits, width // count
    piece = rows // seq
    slots = bits + 5
    dma = pltpu.SemaphoreType.DMA
    steps = 1 + bits + (chips - 1).bit_length()
    out, _, small_out = pl.pallas_call(
        functools.partial(reduce_kernel, chips, bits, count),
        out_shape=(
            jax.ShapeDtypeStruct((rows, width), BF16),
            jax.ShapeDtypeStruct((count, chips, rows, wide), BF16),
            jax.ShapeDtypeStruct(small.shape, F32),
        ),
        in_specs=[pl.BlockSpec(memory_space=pl.ANY), pl.BlockSpec(memory_space=pltpu.VMEM)],
        out_specs=(
            pl.BlockSpec(memory_space=pl.ANY),
            pl.BlockSpec(memory_space=pl.ANY),
            pl.BlockSpec(memory_space=pltpu.VMEM),
        ),
        scratch_shapes=[pltpu.VMEM((count, chips, rows >> (step + 1), wide), BF16) for step in range(bits)]
        + [
            pltpu.VMEM((slots, chips, rows, wide), BF16),
            pltpu.VMEM((2, chips, rows, wide), BF16),
            pltpu.VMEM((count, chips - 1, piece, wide), BF16),
            pltpu.VMEM((count, piece, wide), BF16),
            dma((count,)),
            dma((count,)),
            dma((count,)),
            dma((count,)),
            dma((count, bits)),
            dma((count, bits)),
            dma((count, chips - 1)),
            dma((count, chips - 1)),
            dma((count, seq - 1)),
            dma((count, seq - 1)),
            dma((count,)),
            pltpu.VMEM((steps + 1,) + small.shape, F32),
            pltpu.VMEM((steps,) + small.shape, F32),
            dma((steps,)),
            dma((steps,)),
        ],
        compiler_params=pltpu.CompilerParams(
            collective_id=number, has_side_effects=True, vmem_limit_bytes=62 * 1024 * 1024
        ),
        cost_estimate=pl.CostEstimate(flops=0, bytes_accessed=800_000_000, transcendentals=0),
    )(terms.reshape(chips, 2, rows, width), small)
    return out, small_out


def gather_kernel(chips, bits, units, weights, ahead, *refs):
    shards, wholes = refs[:weights], refs[weights : 2 * weights]
    held = refs[2 * weights : 3 * weights]
    (in_sem, own_sem, along_out, along_in, spread_out, spread_in, turn_out, turn_in) = refs[3 * weights :]
    here = Place(chips, bits)
    seq = 1 << bits

    barrier = pltpu.get_barrier_semaphore()
    peers = [here.sibling()] + [here.partner(i) for i in range(bits)] + [here.chip(k) for k in range(1, chips)]
    for peer in peers:
        pl.semaphore_signal(barrier, inc=1, device_id=peer, device_id_type=pl.DeviceIdType.MESH)
    pl.semaphore_wait(barrier, len(peers))

    def rows_of(unit, shift):
        which, first, width = units[unit]
        count = shards[which].shape[0]
        row = (((here.z - shift) % chips) * 2 + here.core) * count
        return which, row, count, first, width

    def piece_of(unit, shift, subset):
        which, row, count, first, width = rows_of(unit, shift)
        part = here.part_of(subset)
        if (count // seq) % 16 == 0:
            size = count // seq
            return which, pl.ds(pl.multiple_of(row + part * size, 16), size), pl.ds(first, width)
        size = width // seq
        return which, pl.ds(pl.multiple_of(row, 16), count), pl.ds(pl.multiple_of(first + part * size, 128), size)

    def remote(source, target, sems, index, device):
        return pltpu.make_async_remote_copy(
            src_ref=source,
            dst_ref=target,
            send_sem=sems[0].at[index],
            recv_sem=sems[1].at[index],
            device_id=device,
            device_id_type=pl.DeviceIdType.MESH,
        )

    def along(unit, k):
        which, row, count, first, width = rows_of(unit, 0)
        _, there, columns = piece_of(unit, 0, 0)
        part = here.part
        if (count // seq) % 16 == 0:
            size = count // seq
            source = shards[which].at[pl.ds(pl.multiple_of(part * size, 16), size), columns]
        else:
            source = shards[which].at[:, columns]
        return remote(source, wholes[which].at[there, columns], (along_out, along_in), (unit, k - 1), here.chip(k))

    def spread(unit, k, subset):
        last = subset.bit_length() - 1
        which, there, columns = piece_of(unit, k, subset ^ (1 << last))
        region = wholes[which].at[there, columns]
        return remote(region, region, (spread_out, spread_in), (unit, k - 1, subset - 1), here.partner(last))

    def turn(unit, k):
        which, row, count, first, width = rows_of(unit, k)
        there = pl.ds(pl.multiple_of(row, 16), count)
        region = wholes[which].at[there, pl.ds(first, width)]
        source = region if k else shards[which].at[:, pl.ds(first, width)]
        return remote(source, region, (turn_out, turn_in), (unit, k), here.sibling())

    def load(which):
        return pltpu.make_async_copy(shards[which], held[which], in_sem.at[which])

    def store(which):
        count = shards[which].shape[0]
        row = (here.z * 2 + here.core) * count
        there = pl.ds(pl.multiple_of(row, 16), count)
        return pltpu.make_async_copy(held[which], wholes[which].at[there], own_sem.at[which])

    def level(size):
        return [subset for subset in range(1, seq) if bin(subset).count("1") == size]

    shifts = range(1, chips)

    def begin(unit):
        for k in shifts:
            along(unit, k).start()
        turn(unit, 0).start()

    def arrive(unit):
        for k in shifts:
            along(unit, k).wait()
            for subset in level(1):
                spread(unit, k, subset).start()

    def pass_on(unit, size):
        for k in shifts:
            for subset in level(size):
                spread(unit, k, subset).wait()
            for subset in level(size + 1):
                spread(unit, k, subset).start()
            if size == bits:
                turn(unit, k).start()

    def finish(unit):
        for k in range(chips):
            turn(unit, k).wait()

    for which in range(weights):
        load(which).start()
    stages = [arrive]
    for size in range(1, bits + 1):
        stages.append(lambda unit, size=size: pass_on(unit, size))
    stages.append(finish)
    for unit in range(min(ahead, len(units))):
        begin(unit)
    for now in range(len(units) + len(stages) - 1):
        if now + ahead < len(units):
            begin(now + ahead)
        for number, stage in enumerate(stages):
            unit = now - number
            if 0 <= unit < len(units):
                stage(unit)
        if now < weights:
            load(now).wait()
            store(now).start()
    for which in range(weights):
        if which >= len(units) + len(stages) - 1:
            load(which).wait()
            store(which).start()
    for which in range(weights):
        store(which).wait()


def gathered(shards, chips, bits, units, ahead):
    weights, seq, count = len(shards), 1 << bits, len(units)
    dma = pltpu.SemaphoreType.DMA
    return pl.pallas_call(
        functools.partial(gather_kernel, chips, bits, units, weights, ahead),
        out_shape=tuple(jax.ShapeDtypeStruct((2 * chips * one.shape[0], one.shape[1]), one.dtype) for one in shards),
        in_specs=[pl.BlockSpec(memory_space=pl.ANY)] * weights,
        out_specs=tuple(pl.BlockSpec(memory_space=pl.ANY) for _ in shards),
        scratch_shapes=[pltpu.VMEM(one.shape, one.dtype) for one in shards]
        + [
            dma((weights,)),
            dma((weights,)),
            dma((count, chips - 1)),
            dma((count, chips - 1)),
            dma((count, chips - 1, seq - 1)),
            dma((count, chips - 1, seq - 1)),
            dma((count, chips)),
            dma((count, chips)),
        ],
        compiler_params=pltpu.CompilerParams(
            collective_id=1, has_side_effects=True, vmem_limit_bytes=62 * 1024 * 1024
        ),
        cost_estimate=pl.CostEstimate(flops=0, bytes_accessed=900_000_000, transcendentals=0),
    )(*shards)


def parts_of(which, width, count):
    return tuple((which, i * (width // count), width // count) for i in range(count))


def scatter_rows(terms):
    return lax.psum_scatter(terms, "batch", scatter_dimension=0, tiled=True)


def local(
    tokens,
    cotangent,
    segment_ids,
    positions,
    attn_gain,
    qkv_weight,
    out_weight,
    mlp_gain,
    gate_up_weight,
    down_weight,
):
    seq = lax.axis_size("seq")
    chips = lax.axis_size("batch") // 2
    bits = seq.bit_length() - 1
    s = lax.axis_index("seq")
    swap = [(i, i ^ 1) for i in range(seq)]
    model_width = tokens.shape[2]
    rows = tokens.shape[1]
    if rows * 2 != DOC_MAX:
        raise ValueError("token shard")
    share = H // KV
    kv_width = KV * HD
    scale_factor = HD ** (-0.5)
    ff_width = gate_up_weight.shape[1] // 2

    shards = (qkv_weight, out_weight, gate_up_weight, down_weight)
    cuts = (2, 2, 8, max(1, min(4, model_width // (seq * 128))))
    units = sum((parts_of(i, one.shape[1], n) for i, (one, n) in enumerate(zip(shards, cuts))), ())
    qkv_whole, out_whole, gate_up_whole, down_whole = gathered(shards, chips, bits, units, 3)

    inputs = tokens[0].astype(F32)
    normed, inv_first = rms_parts(inputs, attn_gain)
    normed_low = normed.astype(BF16)
    projected = dot(normed_low, qkv_whole)

    row_start = s * rows
    own_segments = lax.dynamic_slice_in_dim(segment_ids[0], row_start, rows, 0)
    other = s ^ 1
    other_segments = lax.dynamic_slice_in_dim(segment_ids[0], other * rows, rows, 0)
    own_positions = lax.dynamic_slice_in_dim(positions[0], row_start, rows, 0)
    cosine, sine_part = rotary_tables(own_positions, HD)
    queries = projected[:, :model_width].astype(BF16).reshape(rows, H, HD)
    queries_rot = rotate(queries.astype(F32), cosine, sine_part).astype(BF16)
    queries_rot = queries_rot.reshape(rows, KV, share, HD)
    keys = projected[:, model_width : model_width + kv_width].astype(BF16).reshape(rows, KV, HD)
    keys_rot = rotate(keys.astype(F32), cosine, sine_part).astype(BF16).reshape(rows, kv_width)
    values = projected[:, model_width + kv_width :].astype(BF16)
    own_kv = jnp.concatenate([keys_rot, values], axis=1)
    other_kv = lax.ppermute(own_kv, "seq", swap)
    both_kv = jnp.concatenate([own_kv, other_kv], axis=0)
    all_keys = both_kv[:, :kv_width].reshape(2 * rows, KV, HD)
    all_values = both_kv[:, kv_width:].reshape(2 * rows, KV, HD)
    index = jnp.arange(rows, dtype=jnp.int32)
    allowed = jnp.concatenate(
        [
            (index[None, :] <= index[:, None]) & (own_segments[None, :] == own_segments[:, None]),
            (other < s) & (other_segments[None, :] == own_segments[:, None]),
        ],
        axis=1,
    )
    scores = (
        jnp.einsum("qgsd,kgd->gsqk", queries_rot, all_keys, preferred_element_type=F32)
        * scale_factor
    )
    masked = jnp.where(allowed[None, None], scores, -1e30)
    row_max = jnp.max(masked, axis=-1, keepdims=True)
    exps = jnp.exp(masked - row_max)
    probs = exps / jnp.sum(exps, axis=-1, keepdims=True)
    probs_low = probs.astype(BF16)
    attended = jnp.einsum("gsqk,kgd->qgsd", probs_low, all_values, preferred_element_type=F32)
    attended = attended.astype(BF16).reshape(rows, model_width)
    residual = inputs + dot(attended, out_whole)
    normed_mlp, inv_second = rms_parts(residual, mlp_gain)
    normed_mlp_low = normed_mlp.astype(BF16)
    gate_up = dot(normed_mlp_low, gate_up_whole)
    gate_part = gate_up[:, :ff_width]
    up_part = gate_up[:, ff_width:]
    sigmoid_gate = jax.nn.sigmoid(gate_part)
    hidden_low = (gate_part * sigmoid_gate * up_part).astype(BF16)

    grad_out = cotangent[0].astype(F32)
    grad_down = cotangent[0]
    early = model_width * 4 // 8
    early_terms = dot_tn(hidden_low, grad_down[:, :early]).astype(BF16)
    early_terms, grad_down = lax.optimization_barrier((early_terms, grad_down))
    down_early = scatter_rows(early_terms)
    grad_hidden = dot_nt(grad_down, down_whole)
    grad_gate = grad_hidden * up_part * sigmoid_gate * (1.0 + gate_part * (1.0 - sigmoid_gate))
    grad_up = grad_hidden * gate_part * sigmoid_gate
    grad_gate_up = jnp.concatenate([grad_gate, grad_up], axis=1).astype(BF16)
    gate_up_terms = dot_tn(normed_mlp_low, grad_gate_up).astype(BF16)
    grad_normed_mlp = dot_nt(grad_gate_up, gate_up_whole)
    mlp_term = jnp.sum(grad_normed_mlp * residual * inv_second, axis=0)
    grad_resid = grad_out + norm_back(grad_normed_mlp, residual, inv_second, mlp_gain)
    grad_proj = grad_resid.astype(BF16)
    out_part = scatter_rows(dot_tn(attended, grad_proj).astype(BF16))
    grad_heads = dot_nt(grad_proj, out_whole)
    grad_heads = grad_heads.astype(BF16).reshape(rows, KV, share, HD)

    grad_probs = jnp.einsum("qgsd,kgd->gsqk", grad_heads, all_values, preferred_element_type=F32)
    inner_sum = jnp.sum(probs * grad_probs, axis=-1, keepdims=True)
    grad_scores = (probs * (grad_probs - inner_sum)).astype(BF16)
    grad_queries = (
        jnp.einsum("gsqk,kgd->qgsd", grad_scores, all_keys, preferred_element_type=F32)
        * scale_factor
    )
    grad_keys = (
        jnp.einsum("gsqk,qgsd->kgd", grad_scores, queries_rot, preferred_element_type=F32)
        * scale_factor
    )
    grad_values = jnp.einsum("gsqk,qgsd->kgd", probs_low, grad_heads, preferred_element_type=F32)
    grad_kv = jnp.concatenate(
        [grad_keys.reshape(2 * rows, kv_width), grad_values.reshape(2 * rows, kv_width)], axis=1
    )
    away = grad_kv[rows:].astype(BF16)
    arrived = lax.ppermute(away, "seq", swap)
    own_grad_kv = grad_kv[:rows] + arrived.astype(F32)
    back_queries = rotate(grad_queries.reshape(rows, H, HD), cosine, -sine_part)
    back_keys = rotate(own_grad_kv[:, :kv_width].reshape(rows, KV, HD), cosine, -sine_part)
    grad_qkv = jnp.concatenate(
        [
            back_queries.reshape(rows, model_width),
            back_keys.reshape(rows, kv_width),
            own_grad_kv[:, kv_width:],
        ],
        axis=1,
    ).astype(BF16)
    qkv_terms, down_early = lax.optimization_barrier((dot_tn(normed_low, grad_qkv).astype(BF16), down_early))
    qkv_part = scatter_rows(qkv_terms)
    def finish(grad_qkv):
        grad_normed = dot_nt(grad_qkv, qkv_whole)
        attn_term = jnp.sum(grad_normed * inputs * inv_first, axis=0)
        back = norm_back(grad_normed, inputs, inv_first, attn_gain)
        gains = jnp.concatenate([attn_term, mlp_term]).reshape(-1, 128)
        return (grad_resid + back).astype(BF16), gains

    two = down_weight.shape[0] // seq % 16 == 0
    gains = jnp.zeros((8, 128), F32)
    if not two:
        tokens_grad, gains = finish(grad_qkv)
    gate_up_grad, gains = reduced(gate_up_terms, gains, chips, bits, 11, 0)
    gate_up_grad, down_early, out_part, qkv_part, hidden_low, grad_qkv = lax.optimization_barrier(
        (gate_up_grad, down_early, out_part, qkv_part, hidden_low, grad_qkv)
    )
    output = (residual + dot(hidden_low, down_whole)).astype(BF16)
    down_terms = dot_tn(hidden_low, grad_down[:, early:]).astype(BF16)
    if two:
        tokens_grad, gains = finish(grad_qkv)
        down_late, gains = reduced(down_terms, gains, chips, bits, 4, 2)
    else:
        down_late = lax.psum(scatter_rows(down_terms), "seq")
    gains = gains.reshape(-1)
    down_early, out_grad, qkv_grad = lax.psum((down_early, out_part, qkv_part), "seq")
    down_grad = jnp.concatenate([down_early, down_late], axis=1)
    return (
        output[None],
        tokens_grad[None],
        gains[:model_width],
        qkv_grad.astype(F32),
        out_grad.astype(F32),
        gains[model_width:],
        gate_up_grad.astype(F32),
        down_grad.astype(F32),
    )


def solution(mesh):
    return jax.shard_map(
        local,
        mesh=mesh,
        in_specs=(
            P("batch", "seq", None),
            P("batch", "seq", None),
            P("batch", None),
            P("batch", None),
            P(),
            P("batch", None),
            P("batch", None),
            P(),
            P("batch", None),
            P("batch", None),
        ),
        out_specs=(
            P("batch", "seq", None),
            P("batch", "seq", None),
            P(),
            P("batch", None),
            P("batch", None),
            P(),
            P("batch", None),
            P("batch", None),
        ),
        check_vma=False,
    )
```
